32 devices in a mesh: day: 4 (over x, core), row: 8 (over z, y).
Axes of the slice: x: 2, y: 2, z: 4, core: 2. Of those that a mesh axis runs over, the one named last changes fastest.
Arguments:
- field: float32 [128, 1024, 1024], P('day', 'row'), may hold values from -6 to 6
- basis_day: float32 [128, 128], replicated, as said below
- basis_x: float32 [1024, 1024], replicated, as said below
- basis_y: float32 [1024, 1024], replicated, as said below
- eig_day: float32 [128], replicated, may hold values from 0.05 to 3
- eig_x: float32 [1024], replicated, may hold values from 0.05 to 3
- eig_y: float32 [1024], replicated, may hold values from 0.05 to 3
- noise: float32 [1], replicated, may hold values from 0.1 to 0.5
Outputs:
- weights: float32 [128, 1024, 1024], P('day', 'row')
The draws below stay inside these ranges and needn't reach their ends.
Inputs may be any that keep to these rules, and one draw needn't show every extreme that they name: basis_day is orthogonal. basis_x is orthogonal. basis_y is orthogonal.
All inputs are finite; a program needn't handle non-finite values.
Results may differ from the reference program's by a relative error of at most 0.00007.
Values sent between devices are 32-bit elements; how exact they have to be, the bound alone decides.
A program may use at most 128 MiB of HBM per device.

```python
import math
import jax
import jax.numpy as jnp
from jax import lax

DAYS = 128
NX = 1024
NY = 1024


def orthogonal(key, order):
    matrix = jax.random.normal(key, (order, order), jnp.float32)
    factor, upper = jnp.linalg.qr(matrix)
    return factor


def draw_basis_day(key, part):
    return orthogonal(jax.random.fold_in(key, 11), DAYS)


def draw_basis_x(key, part):
    return orthogonal(jax.random.fold_in(key, 23), NX)


def draw_basis_y(key, part):
    return orthogonal(jax.random.fold_in(key, 37), NY)


def levels(own_key, shape, cuts, low, high):
    def one(position, parts):
        draws = jax.random.uniform(jax.random.fold_in(jax.random.fold_in(own_key, 6), position), (parts,), jnp.float32, low / len(cuts), high / len(cuts))
        return jnp.repeat(jnp.exp(draws), shape[position] // parts).reshape((-1,) + (1,) * (len(shape) - position - 1))

    loudness = one(*cuts[0])
    for cut in cuts[1:]:
        loudness = loudness * one(*cut)
    return loudness


def normal_values(rng, extent, deviation, limit, pieces=(), kind=jnp.bfloat16):
    loudness = levels(rng, extent, pieces, -0.22, 0.18) if pieces else 1.0
    result = jax.random.normal(rng, extent, jnp.float32) * deviation * loudness
    return jnp.minimum(jnp.maximum(result, -limit), limit).astype(kind)


def setup_inputs(seed: int = 0) -> dict:
    key_of = jax.random.split(jax.random.key(seed), 9)
    return {
        "field": normal_values(key_of[0], (DAYS, NX, NY), 1.0, 6.0, ((0, 4), (1, 8)), jnp.float32),
        "basis_day": draw_basis_day(jax.random.fold_in(key_of[8], 71), 0),
        "basis_x": draw_basis_x(jax.random.fold_in(key_of[8], 71), 0),
        "basis_y": draw_basis_y(jax.random.fold_in(key_of[8], 71), 0),
        "eig_day": jnp.clip(jnp.exp(jax.random.uniform(key_of[4], (DAYS,), jnp.float32, math.log(0.05), math.log(3.0))), 0.05, 3.0),
        "eig_x": jnp.clip(jnp.exp(jax.random.uniform(key_of[5], (NX,), jnp.float32, math.log(0.05), math.log(3.0))), 0.05, 3.0),
        "eig_y": jnp.clip(jnp.exp(jax.random.uniform(key_of[6], (NY,), jnp.float32, math.log(0.05), math.log(3.0))), 0.05, 3.0),
        "noise": jnp.clip(jnp.exp(jax.random.uniform(key_of[7], (1,), jnp.float32, math.log(0.1), math.log(0.5))), 0.1, 0.5),
    }


def reference(field, basis_day, basis_x, basis_y, eig_day, eig_x, eig_y, noise):
    precise = lax.Precision.HIGHEST
    along_y = jnp.einsum('txy,yb->txb', field, basis_y, precision=precise)
    along_x = jnp.einsum('txb,xa->tab', along_y, basis_x, precision=precise)
    spectral = jnp.einsum('tab,ts->sab', along_x, basis_day, precision=precise)
    spectrum = eig_day[:, None, None] * eig_x[None, :, None] * eig_y[None, None, :] + noise[0]
    scaled = spectral / spectrum
    back_day = jnp.einsum('sab,ts->tab', scaled, basis_day, precision=precise)
    back_x = jnp.einsum('tab,xa->txb', back_day, basis_x, precision=precise)
    return jnp.einsum('txb,yb->txy', back_x, basis_y, precision=precise)
```

```python
import functools
import jax
import jax.numpy as jnp
from jax import lax
from jax.experimental import pallas as pl
from jax.experimental.pallas import tpu as pltpu
from jax.sharding import PartitionSpec as P

CHUNKS = 4
SUB = 8
LANES = 128
TILE = 256
MESH = pl.DeviceIdType.MESH


def split(value):
    high = value.astype(jnp.bfloat16)
    low = (value - high.astype(jnp.float32)).astype(jnp.bfloat16)
    return high, low


def dot3(left, right):
    def one(a, b):
        return jnp.dot(a, b, preferred_element_type=jnp.float32)

    return one(left[0], right[0]) + (one(left[0], right[1]) + one(left[1], right[0]))


def flipped(index, mask, size):
    total, bit = 0, 1
    while bit < size:
        total = total + bit * ((index // bit + mask // bit) % 2)
        bit *= 2
    return total


def block(start, size):
    return pl.ds(pl.multiple_of(start * size, size), size)


def each(count, fn):
    def step(i, carry):
        fn(i)
        return carry

    lax.fori_loop(0, count, step, 0)


def kernel(
    field, basis_day, basis_x, basis_y, eig_day, eig_x, eig_y, noise,
    out, send_a, recv_a, send_b, recv_b,
    y_high, y_low, yt_high, yt_low, x_high, x_low, xt_high, xt_low,
    day_high, day_low, dayt_high, dayt_low, day_col,
    big, sheets, left_high, left_low, stage, tall_high, tall_low,
    load_sem, y_sem, x_sem, local_sem, own_sem, out_sem,
    a_send, a_recv, b_send, b_recv,
):
    days = lax.axis_size("day")
    rows = lax.axis_size("row")
    day = lax.axis_index("day")
    row = lax.axis_index("row")
    peers = days * rows
    me = day * rows + row
    chunks, _, depth, own_rows = recv_a.shape
    cols = peers * SUB
    tiles, height, order = big.shape[0], big.shape[1], big.shape[2]
    span = height // own_rows
    steps = depth // (span * SUB)
    piece = span * SUB
    total_days = basis_day.shape[0]

    barrier = pltpu.get_barrier_semaphore()

    def peer(q):
        mask = peers - 1 - q
        to_row = flipped(row, mask // days, rows)
        to_day = flipped(day, mask % days, days)
        return to_day, to_row

    def greet(q):
        pl.semaphore_signal(barrier, inc=1, device_id=peer(q), device_id_type=MESH)

    def load_field(n, slot):
        return pltpu.make_async_copy(field.at[block(n % steps, height)], big.at[slot], load_sem.at[slot])

    def load_y(k):
        return pltpu.make_async_copy(basis_y.at[:, block(k, cols)], big.at[3, :, block(k, cols)], y_sem.at[k])

    load_y(0).start()
    load_field(0, 0).start()
    each(chunks - 1, lambda k: load_y(k + 1).start())
    load_x = pltpu.make_async_copy(basis_x, big.at[2], x_sem)
    load_x.start()
    each(peers - 1, greet)
    pl.semaphore_wait(barrier, peers - 1)

    def prepare_y(k):
        load_y(k).wait()

        def part(i):
            high, low = split(big[3, block(i, TILE), block(k, cols)])
            y_high[k, block(i, TILE), :] = high
            y_low[k, block(i, TILE), :] = low

        each(order // TILE, part)

    def split_rows(slot):
        def part(i):
            high, low = split(big[slot, block(i, TILE // 4), :])
            left_high[block(i, TILE // 4), :] = high
            left_low[block(i, TILE // 4), :] = low

        each(height // (TILE // 4), part)

    def forward(n):
        k = n // steps
        tau = n % steps
        slot = n % 2

        @pl.when(tau == 0)
        def _():
            prepare_y(k)

        load_field(n, slot).wait()

        @pl.when(n + 1 < chunks * steps)
        def _():
            load_field(n + 1, (n + 1) % 2).start()

        split_rows(slot)

        def part(i):
            left = left_high[block(i, TILE), :], left_low[block(i, TILE), :]
            value = dot3(left, (y_high[k], y_low[k])).T
            for j in range(TILE // own_rows):
                one = value[:, j * own_rows : (j + 1) * own_rows].reshape(peers, SUB, own_rows)
                stage[:, block(i * (TILE // own_rows) + j, SUB), :] = one

        each(height // TILE, part)
        here = block(tau, piece)
        copy = pltpu.make_async_copy(stage, send_a.at[k, :, here, :], local_sem)
        own = pltpu.make_async_copy(stage.at[me], recv_a.at[k, me, here, :], own_sem)
        copy.start()
        own.start()
        copy.wait()
        own.wait()

        def send(q):
            to_day, to_row = peer(q)
            pltpu.make_async_remote_copy(
                src_ref=send_a.at[k, to_day * rows + to_row, here, :],
                dst_ref=recv_a.at[k, me, here, :],
                send_sem=a_send.at[k],
                recv_sem=a_recv.at[k],
                device_id=(to_day, to_row),
                device_id_type=MESH,
            ).start()

        each(peers - 1, send)

    each(chunks * steps, forward)

    load_x.wait()

    def turn_y(k):
        def part(i):
            high, low = split(big[3, block(i, TILE), block(k, cols)].T)
            yt_high[k, :, block(i, TILE)] = high
            yt_low[k, :, block(i, TILE)] = low

        each(order // TILE, part)

    each(chunks, turn_y)

    def turn_x(i):
        def part(j):
            value = big[2, block(i, TILE), block(j, TILE)]
            high, low = split(value)
            x_high[block(i, TILE), block(j, TILE)] = high
            x_low[block(i, TILE), block(j, TILE)] = low
            high, low = split(value.T)
            xt_high[block(j, TILE), block(i, TILE)] = high
            xt_low[block(j, TILE), block(i, TILE)] = low

        each(order // TILE, part)

    each(order // TILE, turn_x)
    day_high[...], day_low[...] = split(basis_day[...])
    dayt_high[...], dayt_low[...] = split(basis_day[...].T)
    day_col[...] = jnp.broadcast_to(eig_day[...], (total_days, total_days)).T

    def spread(i, j, value):
        for part in range(TILE // LANES):
            sheets[j * (TILE // LANES) + part, block(i, TILE), :] = value[:, part * LANES : (part + 1) * LANES]

    def settle(i, j, value):
        big[2, block(i, TILE), block(j, TILE)] = value

    def product(put, high, low):
        def part(n):
            i, j = n // (order // TILE), n % (order // TILE)
            left = left_high[block(i, TILE), :], left_low[block(i, TILE), :]
            put(i, j, dot3(left, (high[:, block(j, TILE)], low[:, block(j, TILE)])))

        each((height // TILE) * (order // TILE), part)

    def middle(k):
        rest = recv_a.at[k, pl.ds(0, peers - 1)]
        pltpu.make_async_copy(rest, rest, a_recv.at[k]).wait()

        def gather(n):
            pltpu.make_async_copy(
                recv_a.at[k, n], big.at[0, block(n // rows, depth), block(n % rows, own_rows)], load_sem.at[0]
            ).start()

        each(peers, gather)
        pltpu.make_async_copy(big.at[0], big.at[0], load_sem.at[0]).wait()
        split_rows(0)
        product(spread, x_high, x_low)

        def solve(j):
            shape = eig_x[:, block(j, LANES)]
            for b in range(SUB):
                where = (j, pl.ds(b, total_days, stride=SUB), slice(None))
                spectral = dot3((dayt_high[...], dayt_low[...]), split(sheets[where]))
                level = eig_y[k * cols + me * SUB + b]
                scaled = spectral / (day_col[...] * shape * level + noise[0])
                sheets[where] = dot3((day_high[...], day_low[...]), split(scaled))

        each(order // LANES, solve)

        def rejoin(n):
            i, j = n // (order // LANES), n % (order // LANES)
            high, low = split(sheets[j, block(i, TILE), :])
            left_high[block(i, TILE), block(j, LANES)] = high
            left_low[block(i, TILE), block(j, LANES)] = low

        each((height // TILE) * (order // LANES), rejoin)
        product(settle, xt_high, xt_low)

        def scatter(n):
            pltpu.make_async_copy(
                big.at[2, block(n // rows, depth), block(n % rows, own_rows)], send_b.at[k, n], local_sem
            ).start()

        each(peers, scatter)
        own = pltpu.make_async_copy(big.at[2, block(day, depth), block(row, own_rows)], recv_b.at[k, me], own_sem)
        own.start()
        pltpu.make_async_copy(big.at[2], big.at[2], local_sem).wait()
        own.wait()

        def send(n):
            tau, q = n // (peers - 1), n % (peers - 1)
            to_day, to_row = peer(q)
            here = block(tau, piece)
            pltpu.make_async_remote_copy(
                src_ref=send_b.at[k, to_day * rows + to_row, here, :],
                dst_ref=recv_b.at[k, me, here, :],
                send_sem=b_send.at[k],
                recv_sem=b_recv.at[k, tau],
                device_id=(to_day, to_row),
                device_id_type=MESH,
            ).start()

        each(steps * (peers - 1), send)

    each(chunks, middle)

    def clear(n):
        big[n // (height // TILE), block(n % (height // TILE), TILE), :] = jnp.zeros((TILE, order), jnp.float32)

    each(tiles * (height // TILE), clear)

    def backward(n):
        k = n // steps
        tau = n % steps
        here = block(tau, piece)
        rest = recv_b.at[k, pl.ds(0, peers - 1), here, :]
        pltpu.make_async_copy(rest, rest, b_recv.at[k, tau]).wait()
        load = pltpu.make_async_copy(recv_b.at[k, :, here, :], stage, local_sem)
        load.start()
        load.wait()

        def turn(i):
            high, low = split(stage[:, block(i, SUB), :].reshape(cols, own_rows).T)
            tall_high[block(i, own_rows), :] = high
            tall_low[block(i, own_rows), :] = low

        each(span, turn)

        def part(m):
            i, j = m // (order // TILE), m % (order // TILE)
            left = tall_high[block(i, TILE), :], tall_low[block(i, TILE), :]
            right = yt_high[k, :, block(j, TILE)], yt_low[k, :, block(j, TILE)]
            big[tau, block(i, TILE), block(j, TILE)] += dot3(left, right)

        each((height // TILE) * (order // TILE), part)

        @pl.when(k == chunks - 1)
        def _():
            pltpu.make_async_copy(big.at[tau], out.at[block(tau, height)], out_sem.at[tau]).start()

    each(chunks * steps, backward)

    def finish(tau):
        pltpu.make_async_copy(big.at[tau], out.at[block(tau, height)], out_sem.at[tau]).wait()

    each(steps, finish)

    def drain(k):
        sent = send_a.at[k, pl.ds(0, peers - 1)]
        pltpu.make_async_copy(sent, sent, a_send.at[k]).wait()
        sent = send_b.at[k, pl.ds(0, peers - 1)]
        pltpu.make_async_copy(sent, sent, b_send.at[k]).wait()

    each(chunks, drain)


def fused(field, basis_day, basis_x, basis_y, eig_day, eig_x, eig_y, noise):
    own_days, own_rows, order = field.shape
    peers = lax.axis_size("day") * lax.axis_size("row")
    total_days = basis_day.shape[0]
    chunks = order // (peers * SUB)
    height = total_days * SUB
    span = height // own_rows
    steps = own_days // span
    depth = own_days * SUB
    f32, bf16 = jnp.float32, jnp.bfloat16
    wire = jax.ShapeDtypeStruct((chunks, peers, depth, own_rows), f32)
    anywhere = pl.BlockSpec(memory_space=pl.ANY)
    vmem = pl.BlockSpec(memory_space=pltpu.VMEM)
    smem = pl.BlockSpec(memory_space=pltpu.SMEM)
    cols = peers * SUB
    dma = pltpu.SemaphoreType.DMA
    square = pltpu.VMEM((order, order), bf16)
    small = pltpu.VMEM((total_days, total_days), bf16)
    result = pl.pallas_call(
        kernel,
        out_shape=(jax.ShapeDtypeStruct((own_days * own_rows, order), f32), wire, wire, wire, wire),
        in_specs=[anywhere, vmem, anywhere, anywhere, vmem, vmem, smem, smem],
        out_specs=(anywhere,) * 5,
        scratch_shapes=[
            pltpu.VMEM((chunks, order, cols), bf16),
            pltpu.VMEM((chunks, order, cols), bf16),
            pltpu.VMEM((chunks, cols, order), bf16),
            pltpu.VMEM((chunks, cols, order), bf16),
            square, square, square, square,
            small, small, small, small,
            pltpu.VMEM((total_days, total_days), f32),
            pltpu.VMEM((steps, height, order), f32),
            pltpu.VMEM((order // LANES, height, LANES), f32),
            pltpu.VMEM((height, order), bf16),
            pltpu.VMEM((height, order), bf16),
            pltpu.VMEM((peers, span * SUB, own_rows), f32),
            pltpu.VMEM((height, cols), bf16),
            pltpu.VMEM((height, cols), bf16),
            dma((2,)), dma((chunks,)), dma, dma, dma, dma((steps,)),
            dma((chunks,)), dma((chunks,)), dma((chunks,)), dma((chunks, steps)),
        ],
        compiler_params=pltpu.CompilerParams(
            collective_id=0, has_side_effects=True, vmem_limit_bytes=60 * 1024 * 1024
        ),
    )(
        field.reshape(own_days * own_rows, order), basis_day, basis_x, basis_y,
        eig_day.reshape(1, -1), eig_x.reshape(1, -1), eig_y, noise,
    )
    return result[0].reshape(field.shape)


def fits(field, basis_day, basis_x):
    own_days, own_rows, order = field.shape
    days, rows = lax.axis_size("day"), lax.axis_size("row")
    peers = days * rows
    height = basis_day.shape[0] * SUB
    return (
        days & (days - 1) == 0
        and rows & (rows - 1) == 0
        and own_rows == LANES
        and basis_day.shape[0] == LANES
        and order % (peers * SUB) == 0
        and peers * SUB == TILE
        and basis_x.shape[0] == order
        and height == order
        and own_days * own_rows == 4 * height
    )


def shift(block, axis, step):
    size = lax.axis_size(axis)
    if step % size == 0:
        return block
    return lax.ppermute(block, axis, [(i, (i + step) % size) for i in range(size)])


def rolled(array, dim, blocks, first, sign):
    width = array.shape[dim] // blocks
    starts = [((first + sign * j) % blocks) * width for j in range(blocks)]
    return jnp.concatenate([lax.dynamic_slice_in_dim(array, start, width, dim) for start in starts], axis=dim)


def exchanged(field, basis_day, basis_x, basis_y, eig_day, eig_x, eig_y, noise):
    precise = lax.Precision.HIGH
    days = lax.axis_size("day")
    rows = lax.axis_size("row")
    day = lax.axis_index("day")
    row = lax.axis_index("row")
    local_days, local_rows, grid_cols = field.shape
    grid_rows = basis_x.shape[0]
    own_cols = grid_cols // rows
    own_spec = grid_rows // days
    chunks = max(1, min(CHUNKS, own_cols // 32))
    width = own_cols // chunks

    def product(spec, left, right):
        return jnp.einsum(spec, left, right, precision=precise, preferred_element_type=jnp.float32)

    turn_x = rolled(rolled(basis_x, 0, rows, row, -1), 1, days, day, 1)
    turn_y = rolled(basis_y.T, 0, rows, row, 1).reshape(rows, chunks, width, grid_cols)
    turn_day = rolled(basis_day, 0, days, day, -1)
    part_x = lax.dynamic_slice_in_dim(eig_x, day * own_spec, own_spec)
    part_y = lax.dynamic_slice_in_dim(eig_y, row * own_cols, own_cols)
    parts = []
    for chunk in range(chunks):
        basis = turn_y[:, chunk].reshape(rows * width, grid_cols)
        along_y = product("by,txy->btx", basis, field)
        got = [shift(along_y[j * width : (j + 1) * width], "row", j) for j in range(rows)]
        along_x = product("btx,xa->bta", jnp.concatenate(got, axis=2), turn_x)
        got = [shift(along_x[:, :, j * own_spec : (j + 1) * own_spec], "day", j) for j in range(days)]
        spectral = product("ts,bta->bsa", turn_day, jnp.concatenate(got, axis=1))
        own_y = part_y[chunk * width : (chunk + 1) * width]
        spectrum = eig_day[None, :, None] * part_x[None, None, :] * own_y[:, None, None] + noise[0]
        back_day = product("ts,bsa->bta", turn_day, spectral / spectrum)
        got = [shift(back_day[:, j * local_days : (j + 1) * local_days], "day", -j) for j in range(days)]
        back_x = product("bta,xa->btx", jnp.concatenate(got, axis=2), turn_x)
        got = [shift(back_x[:, :, j * local_rows : (j + 1) * local_rows], "row", -j) for j in range(rows)]
        parts.append((basis, jnp.concatenate(got, axis=0)))
    weights = None
    for group in (parts[:-1], parts[-1:]):
        if group:
            basis = jnp.concatenate([g[0] for g in group], axis=0)
            value = product("btx,by->txy", jnp.concatenate([g[1] for g in group], axis=0), basis)
            weights = value if weights is None else weights + value
    return weights


def body(field, basis_day, basis_x, *rest):
    route = fused if fits(field, basis_day, basis_x) else exchanged
    return route(field, basis_day, basis_x, *rest)


def solution(mesh):
    in_specs = (P("day", "row", None), P(), P(), P(), P(), P(), P(), P())
    out_specs = P("day", "row", None)
    return jax.shard_map(body, mesh=mesh, in_specs=in_specs, out_specs=out_specs, check_vma=False)
```

```python
import functools
import jax
import jax.numpy as jnp
from jax import lax
from jax.experimental import pallas as pl
from jax.experimental.pallas import tpu as pltpu
from jax.sharding import PartitionSpec as P

CHUNKS = 4
SUB = 8
LANES = 128
TILE = 256
MESH = pl.DeviceIdType.MESH


def split(value):
    high = value.astype(jnp.bfloat16)
    low = (value - high.astype(jnp.float32)).astype(jnp.bfloat16)
    return high, low


def dot3(left, right):
    def one(a, b):
        return jnp.dot(a, b, preferred_element_type=jnp.float32)

    return one(left[0], right[0]) + (one(left[0], right[1]) + one(left[1], right[0]))


def flipped(index, mask, size):
    total, bit = 0, 1
    while bit < size:
        total = total + bit * ((index // bit + mask // bit) % 2)
        bit *= 2
    return total


def block(start, size):
    return pl.ds(pl.multiple_of(start * size, size), size)


def each(count, fn):
    def step(i, carry):
        fn(i)
        return carry

    lax.fori_loop(0, count, step, 0)


def kernel(
    field, basis_day, basis_x, basis_y, day_values, x_values, y_values, noise_value,
    total, send_a, recv_a, send_b, recv_b,
    y_high, y_low, yt_high, yt_low, x_high, x_low, xt_high, xt_low,
    day_high, day_low, dayt_high, dayt_low, day_col, day_full, eig_day, eig_x, eig_y, noise,
    sheets, left_high, left_low, stage, tall_high, tall_low,
    load_sem, y_sem, x_sem, small_sem, local_sem, own_sem,
    a_send, a_recv, b_send, b_recv, last_recv,
):
    days = lax.axis_size("day")
    rows = lax.axis_size("row")
    day = lax.axis_index("day")
    row = lax.axis_index("row")
    peers = days * rows
    me = day * rows + row
    chunks, _, depth, own_rows = recv_a.shape
    cols = peers * SUB
    tiles, height, order = total.shape[0], total.shape[1], total.shape[2]
    span = height // own_rows
    steps = depth // (span * SUB)
    piece = span * SUB
    total_days = basis_day.shape[0]

    barrier = pltpu.get_barrier_semaphore()

    def peer(q):
        mask = peers - 1 - q
        to_row = flipped(row, mask // days, rows)
        to_day = flipped(day, mask % days, days)
        return to_day, to_row

    def greet(q):
        pl.semaphore_signal(barrier, inc=1, device_id=peer(q), device_id_type=MESH)

    parts = height // TILE
    fine = piece // parts

    def load_part(n, i):
        source = field.at[block((n % steps) * parts + i, TILE)]
        return pltpu.make_async_copy(source, total.at[n % 2, block(i, TILE)], load_sem.at[n % 2, i])

    def load_field(n):
        each(parts, lambda i: load_part(n, i).start())

    def load_y(k):
        return pltpu.make_async_copy(basis_y.at[:, block(k, cols)], total.at[3, :, block(k, cols)], y_sem.at[k])

    load_y(0).start()
    load_field(0)
    each(chunks - 1, lambda k: load_y(k + 1).start())
    load_x = pltpu.make_async_copy(basis_x, total.at[2], x_sem)
    load_x.start()
    loads = [
        pltpu.make_async_copy(source, target, small_sem.at[i])
        for i, (source, target) in enumerate(
            ((basis_day, day_full), (day_values, eig_day), (x_values, eig_x), (y_values, eig_y), (noise_value, noise))
        )
    ]
    for load in loads:
        load.start()
    each(peers - 1, greet)
    pl.semaphore_wait(barrier, peers - 1)

    def prepare_y(k):
        load_y(k).wait()

        def part(i):
            high, low = split(total[3, block(i, TILE), block(k, cols)])
            y_high[k, block(i, TILE), :] = high
            y_low[k, block(i, TILE), :] = low

        each(order // TILE, part)

    def split_rows(slot, first, count):
        def part(i):
            here = block(first * 4 + i, TILE // 4)
            high, low = split(total[slot, here, :])
            left_high[here, :] = high
            left_low[here, :] = low

        each(count * 4, part)

    def along_y(k, slot, first, count):
        split_rows(slot, first, count)

        def part(i):
            here = block(first + i, TILE)
            value = dot3((left_high[here, :], left_low[here, :]), (y_high[k], y_low[k])).T
            for j in range(TILE // own_rows):
                one = value[:, j * own_rows : (j + 1) * own_rows].reshape(peers, SUB, own_rows)
                stage[:, block(i * (TILE // own_rows) + j, SUB), :] = one

        each(count, part)

    def send_y(k, here, length):
        staged = stage.at[:, pl.ds(0, length), :]
        copy = pltpu.make_async_copy(staged, send_a.at[k, :, here, :], local_sem)
        own = pltpu.make_async_copy(stage.at[me, pl.ds(0, length), :], recv_a.at[k, me, here, :], own_sem)
        copy.start()
        own.start()
        copy.wait()
        own.wait()

        def send(q):
            to_day, to_row = peer(q)
            pltpu.make_async_remote_copy(
                src_ref=send_a.at[k, to_day * rows + to_row, here, :],
                dst_ref=recv_a.at[k, me, here, :],
                send_sem=a_send.at[k],
                recv_sem=a_recv.at[k],
                device_id=(to_day, to_row),
                device_id_type=MESH,
            ).start()

        each(peers - 1, send)

    prepare_y(0)

    def first(i):
        load_part(0, i).wait()
        along_y(0, 0, i, 1)
        send_y(0, block(i, fine), fine)

    each(parts, first)
    load_field(1)

    def forward(m):
        n = m + 1
        k = n // steps

        @pl.when(n % steps == 0)
        def _():
            prepare_y(k)

        each(parts, lambda i: load_part(n, i).wait())

        @pl.when(n + 1 < chunks * steps)
        def _():
            load_field(n + 1)

        along_y(k, n % 2, 0, parts)
        send_y(k, block(n % steps, piece), piece)

    each(chunks * steps - 1, forward)

    for load in loads:
        load.wait()
    load_x.wait()

    def turn_y(k):
        def part(i):
            high, low = split(total[3, block(i, TILE), block(k, cols)].T)
            yt_high[k, :, block(i, TILE)] = high
            yt_low[k, :, block(i, TILE)] = low

        each(order // TILE, part)

    each(chunks, turn_y)

    def turn_x(i):
        def part(j):
            value = total[2, block(i, TILE), block(j, TILE)]
            high, low = split(value)
            x_high[block(i, TILE), block(j, TILE)] = high
            x_low[block(i, TILE), block(j, TILE)] = low
            high, low = split(value.T)
            xt_high[block(j, TILE), block(i, TILE)] = high
            xt_low[block(j, TILE), block(i, TILE)] = low

        each(order // TILE, part)

    each(order // TILE, turn_x)
    day_high[...], day_low[...] = split(day_full[...])
    dayt_high[...], dayt_low[...] = split(day_full[...].T)
    day_col[...] = jnp.broadcast_to(eig_day[...], (total_days, total_days)).T

    def spread(i, j, value):
        for part in range(TILE // LANES):
            sheets[j * (TILE // LANES) + part, block(i, TILE), :] = value[:, part * LANES : (part + 1) * LANES]

    def settle(i, j, value):
        total[2, block(i, TILE), block(j, TILE)] = value

    def product(put, high, low):
        def part(n):
            i, j = n // (order // TILE), n % (order // TILE)
            left = left_high[block(i, TILE), :], left_low[block(i, TILE), :]
            put(i, j, dot3(left, (high[:, block(j, TILE)], low[:, block(j, TILE)])))

        each((height // TILE) * (order // TILE), part)

    def middle(k):
        rest = recv_a.at[k, pl.ds(0, peers - 1)]
        pltpu.make_async_copy(rest, rest, a_recv.at[k]).wait()

        def gather(n):
            pltpu.make_async_copy(
                recv_a.at[k, n], total.at[0, block(n // rows, depth), block(n % rows, own_rows)], local_sem
            ).start()

        each(peers, gather)
        pltpu.make_async_copy(total.at[0], total.at[0], local_sem).wait()
        split_rows(0, 0, parts)
        product(spread, x_high, x_low)

        def solve(j):
            shape = eig_x[:, block(j, LANES)]
            for b in range(SUB):
                where = (j, pl.ds(b, total_days, stride=SUB), slice(None))
                spectral = dot3((dayt_high[...], dayt_low[...]), split(sheets[where]))
                level = eig_y[k * cols + me * SUB + b]
                scaled = spectral / (day_col[...] * shape * level + noise[0])
                sheets[where] = dot3((day_high[...], day_low[...]), split(scaled))

        each(order // LANES, solve)

        def rejoin(n):
            i, j = n // (order // LANES), n % (order // LANES)
            high, low = split(sheets[j, block(i, TILE), :])
            left_high[block(i, TILE), block(j, LANES)] = high
            left_low[block(i, TILE), block(j, LANES)] = low

        each((height // TILE) * (order // LANES), rejoin)
        product(settle, xt_high, xt_low)

        def scatter(n):
            pltpu.make_async_copy(
                total.at[2, block(n // rows, depth), block(n % rows, own_rows)], send_b.at[k, n], local_sem
            ).start()

        each(peers, scatter)
        own = pltpu.make_async_copy(total.at[2, block(day, depth), block(row, own_rows)], recv_b.at[k, me], own_sem)
        own.start()
        pltpu.make_async_copy(total.at[2], total.at[2], local_sem).wait()
        own.wait()

        def send(q, here, arrived):
            to_day, to_row = peer(q)
            pltpu.make_async_remote_copy(
                src_ref=send_b.at[k, to_day * rows + to_row, here, :],
                dst_ref=recv_b.at[k, me, here, :],
                send_sem=b_send.at[k],
                recv_sem=arrived,
                device_id=(to_day, to_row),
                device_id_type=MESH,
            ).start()

        def send_part(n, first, count):
            tau, q = n // count, first + n % count
            send(q, block(tau, piece), b_recv.at[k, tau])

        def send_last(n, first, count):
            i, q = n // count, first + n % count
            send(q, block((steps - 1) * parts + i, fine), last_recv.at[i])

        @pl.when(k < chunks - 1)
        def _():
            each(steps * (peers - 1), lambda n: send_part(n, 0, peers - 1))

        @pl.when(k == chunks - 1)
        def _():
            far, near = peers // 2, peers - 1 - peers // 2
            each((steps - 1) * near, lambda n: send_part(n, far, near))
            each(parts * near, lambda n: send_last(n, far, near))
            each((steps - 1) * far, lambda n: send_part(n, 0, far))
            each(parts * far, lambda n: send_last(n, 0, far))

    each(chunks, middle)

    def clear(n):
        total[n // (height // TILE), block(n % (height // TILE), TILE), :] = jnp.zeros((TILE, order), jnp.float32)

    each(tiles * (height // TILE), clear)

    def along_b(k, tau, here, length, first, count, arrived):
        rest = recv_b.at[k, pl.ds(0, peers - 1), here, :]
        pltpu.make_async_copy(rest, rest, arrived).wait()
        load = pltpu.make_async_copy(recv_b.at[k, :, here, :], stage.at[:, pl.ds(0, length), :], local_sem)
        load.start()
        load.wait()

        def turn(i):
            high, low = split(stage[:, block(i, SUB), :].reshape(cols, own_rows).T)
            tall_high[block(i, own_rows), :] = high
            tall_low[block(i, own_rows), :] = low

        each(length // SUB, turn)

        def part(m):
            i, j = m // (order // TILE), m % (order // TILE)
            left = tall_high[block(i, TILE), :], tall_low[block(i, TILE), :]
            right = yt_high[k, :, block(j, TILE)], yt_low[k, :, block(j, TILE)]
            total[tau, block(first + i, TILE), block(j, TILE)] += dot3(left, right)

        each(count * (order // TILE), part)

    def backward(n):
        k, tau = n // steps, n % steps
        along_b(k, tau, block(tau, piece), piece, 0, parts, b_recv.at[k, tau])

    each(chunks * steps - 1, backward)

    def last(i):
        along_b(chunks - 1, steps - 1, block((steps - 1) * parts + i, fine), fine, i, 1, last_recv.at[i])

    each(parts, last)

    def drain(k):
        sent = send_a.at[k, pl.ds(0, peers - 1)]
        pltpu.make_async_copy(sent, sent, a_send.at[k]).wait()
        sent = send_b.at[k, pl.ds(0, peers - 1)]
        pltpu.make_async_copy(sent, sent, b_send.at[k]).wait()

    each(chunks, drain)


def fused(field, basis_day, basis_x, basis_y, eig_day, eig_x, eig_y, noise):
    own_days, own_rows, order = field.shape
    peers = lax.axis_size("day") * lax.axis_size("row")
    total_days = basis_day.shape[0]
    chunks = order // (peers * SUB)
    height = total_days * SUB
    span = height // own_rows
    steps = own_days // span
    depth = own_days * SUB
    f32, bf16 = jnp.float32, jnp.bfloat16
    wire = jax.ShapeDtypeStruct((chunks, peers, depth, own_rows), f32)
    anywhere = pl.BlockSpec(memory_space=pl.ANY)
    vmem = pl.BlockSpec(memory_space=pltpu.VMEM)
    cols = peers * SUB
    dma = pltpu.SemaphoreType.DMA
    square = pltpu.VMEM((order, order), bf16)
    small = pltpu.VMEM((total_days, total_days), bf16)
    result = pl.pallas_call(
        kernel,
        out_shape=(pltpu.VMEM((steps, height, order), f32), wire, wire, wire, wire),
        in_specs=[pl.BlockSpec(memory_space=pltpu.HBM)] * 8,
        out_specs=(vmem,) + (anywhere,) * 4,
        scratch_shapes=[
            pltpu.VMEM((chunks, order, cols), bf16),
            pltpu.VMEM((chunks, order, cols), bf16),
            pltpu.VMEM((chunks, cols, order), bf16),
            pltpu.VMEM((chunks, cols, order), bf16),
            square, square, square, square,
            small, small, small, small,
            pltpu.VMEM((total_days, total_days), f32),
            pltpu.VMEM((total_days, total_days), f32),
            pltpu.VMEM((1, total_days), f32),
            pltpu.VMEM((1, order), f32),
            pltpu.SMEM((order,), f32),
            pltpu.SMEM((1,), f32),
            pltpu.VMEM((order // LANES, height, LANES), f32),
            pltpu.VMEM((height, order), bf16),
            pltpu.VMEM((height, order), bf16),
            pltpu.VMEM((peers, span * SUB, own_rows), f32),
            pltpu.VMEM((height, cols), bf16),
            pltpu.VMEM((height, cols), bf16),
            dma((2, height // TILE)), dma((chunks,)), dma, dma((5,)), dma, dma,
            dma((chunks,)), dma((chunks,)), dma((chunks,)), dma((chunks, steps)), dma((height // TILE,)),
        ],
        compiler_params=pltpu.CompilerParams(
            collective_id=0, has_side_effects=True, vmem_limit_bytes=44 * 1024 * 1024
        ),
    )(
        field.reshape(own_days * own_rows, order), basis_day, basis_x, basis_y,
        eig_day.reshape(1, -1), eig_x.reshape(1, -1), eig_y, noise,
    )
    return result[0].reshape(field.shape)


def fits(field, basis_day, basis_x):
    own_days, own_rows, order = field.shape
    days, rows = lax.axis_size("day"), lax.axis_size("row")
    peers = days * rows
    height = basis_day.shape[0] * SUB
    return (
        days & (days - 1) == 0
        and rows & (rows - 1) == 0
        and own_rows == LANES
        and basis_day.shape[0] == LANES
        and order % (peers * SUB) == 0
        and peers * SUB == TILE
        and basis_x.shape[0] == order
        and height == order
        and own_days * own_rows == 4 * height
    )


def shift(block, axis, step):
    size = lax.axis_size(axis)
    if step % size == 0:
        return block
    return lax.ppermute(block, axis, [(i, (i + step) % size) for i in range(size)])


def rolled(array, dim, blocks, first, sign):
    width = array.shape[dim] // blocks
    starts = [((first + sign * j) % blocks) * width for j in range(blocks)]
    return jnp.concatenate([lax.dynamic_slice_in_dim(array, start, width, dim) for start in starts], axis=dim)


def exchanged(field, basis_day, basis_x, basis_y, eig_day, eig_x, eig_y, noise):
    precise = lax.Precision.HIGH
    days = lax.axis_size("day")
    rows = lax.axis_size("row")
    day = lax.axis_index("day")
    row = lax.axis_index("row")
    local_days, local_rows, grid_cols = field.shape
    grid_rows = basis_x.shape[0]
    own_cols = grid_cols // rows
    own_spec = grid_rows // days
    chunks = max(1, min(CHUNKS, own_cols // 32))
    width = own_cols // chunks

    def product(spec, left, right):
        return jnp.einsum(spec, left, right, precision=precise, preferred_element_type=jnp.float32)

    turn_x = rolled(rolled(basis_x, 0, rows, row, -1), 1, days, day, 1)
    turn_y = rolled(basis_y.T, 0, rows, row, 1).reshape(rows, chunks, width, grid_cols)
    turn_day = rolled(basis_day, 0, days, day, -1)
    part_x = lax.dynamic_slice_in_dim(eig_x, day * own_spec, own_spec)
    part_y = lax.dynamic_slice_in_dim(eig_y, row * own_cols, own_cols)
    parts = []
    for chunk in range(chunks):
        basis = turn_y[:, chunk].reshape(rows * width, grid_cols)
        along_y = product("by,txy->btx", basis, field)
        got = [shift(along_y[j * width : (j + 1) * width], "row", j) for j in range(rows)]
        along_x = product("btx,xa->bta", jnp.concatenate(got, axis=2), turn_x)
        got = [shift(along_x[:, :, j * own_spec : (j + 1) * own_spec], "day", j) for j in range(days)]
        spectral = product("ts,bta->bsa", turn_day, jnp.concatenate(got, axis=1))
        own_y = part_y[chunk * width : (chunk + 1) * width]
        spectrum = eig_day[None, :, None] * part_x[None, None, :] * own_y[:, None, None] + noise[0]
        back_day = product("ts,bsa->bta", turn_day, spectral / spectrum)
        got = [shift(back_day[:, j * local_days : (j + 1) * local_days], "day", -j) for j in range(days)]
        back_x = product("bta,xa->btx", jnp.concatenate(got, axis=2), turn_x)
        got = [shift(back_x[:, :, j * local_rows : (j + 1) * local_rows], "row", -j) for j in range(rows)]
        parts.append((basis, jnp.concatenate(got, axis=0)))
    weights = None
    for group in (parts[:-1], parts[-1:]):
        if group:
            basis = jnp.concatenate([g[0] for g in group], axis=0)
            value = product("btx,by->txy", jnp.concatenate([g[1] for g in group], axis=0), basis)
            weights = value if weights is None else weights + value
    return weights


def body(field, basis_day, basis_x, *rest):
    route = fused if fits(field, basis_day, basis_x) else exchanged
    return route(field, basis_day, basis_x, *rest)


def solution(mesh):
    in_specs = (P("day", "row", None), P(), P(), P(), P(), P(), P(), P())
    out_specs = P("day", "row", None)
    return jax.shard_map(body, mesh=mesh, in_specs=in_specs, out_specs=out_specs, check_vma=False)
```

```python
import functools
import jax
import jax.numpy as jnp
from jax import lax
from jax.experimental import pallas as pl
from jax.experimental.pallas import tpu as pltpu
from jax.sharding import PartitionSpec as P

CHUNKS = 4
SUB = 8
LANES = 128
TILE = 256
SPLIT = 2
MESH = pl.DeviceIdType.MESH


def split(value):
    high = value.astype(jnp.bfloat16)
    low = (value - high.astype(jnp.float32)).astype(jnp.bfloat16)
    return high, low


def dot3(left, right):
    def one(a, b):
        return jnp.dot(a, b, preferred_element_type=jnp.float32)

    return one(left[0], right[0]) + (one(left[0], right[1]) + one(left[1], right[0]))


def flipped(index, mask, size):
    total, bit = 0, 1
    while bit < size:
        total = total + bit * ((index // bit + mask // bit) % 2)
        bit *= 2
    return total


def block(start, size):
    return pl.ds(pl.multiple_of(start * size, size), size)


def each(count, fn):
    def step(i, carry):
        fn(i)
        return carry

    lax.fori_loop(0, count, step, 0)


def kernel(
    field, basis_day, basis_x, basis_y, day_values, x_values, y_values, noise_value,
    total, send_a, recv_a, send_b, recv_b,
    y_high, y_low, yt_high, yt_low, x_high, x_low, xt_high, xt_low,
    day_high, day_low, dayt_high, dayt_low, day_col, day_full, eig_day, eig_x, eig_y, noise,
    sheets, left_high, left_low, stage, tall_high, tall_low,
    load_sem, y_sem, x_sem, small_sem, local_sem, own_sem,
    a_send, a_recv, b_send, b_recv, last_recv,
):
    days = lax.axis_size("day")
    rows = lax.axis_size("row")
    day = lax.axis_index("day")
    row = lax.axis_index("row")
    peers = days * rows
    me = day * rows + row
    chunks, _, depth, own_rows = recv_a.shape
    cols = peers * SUB
    tiles, height, order = total.shape[0], total.shape[1], total.shape[2]
    span = height // own_rows
    steps = depth // (span * SUB)
    piece = span * SUB
    total_days = basis_day.shape[0]

    barrier = pltpu.get_barrier_semaphore()

    def peer(q):
        half = peers // 2
        near = q // half
        mask = (1 - near) * (half + q) + near * (peers - 1 - q)
        i, j = mask // days, mask % days
        to_row = flipped(row, i, rows)
        to_day = flipped(day, j, days)
        return to_day, to_row

    def greet(q):
        pl.semaphore_signal(barrier, inc=1, device_id=peer(q), device_id_type=MESH)

    parts = height // TILE
    fine = piece // parts

    def load_part(n, i):
        source = field.at[block((n % steps) * parts + i, TILE)]
        return pltpu.make_async_copy(source, total.at[n % 2, block(i, TILE)], load_sem.at[n % 2, i])

    def load_field(n):
        each(parts, lambda i: load_part(n, i).start())

    def load_y(k):
        return pltpu.make_async_copy(basis_y.at[:, block(k, cols)], total.at[3, :, block(k, cols)], y_sem.at[k])

    load_y(0).start()
    load_field(0)
    each(chunks - 1, lambda k: load_y(k + 1).start())
    load_x = pltpu.make_async_copy(basis_x, total.at[2], x_sem)
    load_x.start()
    loads = [
        pltpu.make_async_copy(source, target, small_sem.at[i])
        for i, (source, target) in enumerate(
            ((basis_day, day_full), (day_values, eig_day), (x_values, eig_x), (y_values, eig_y), (noise_value, noise))
        )
    ]
    for load in loads:
        load.start()
    each(peers - 1, greet)
    pl.semaphore_wait(barrier, peers - 1)

    def prepare_y(k):
        load_y(k).wait()

        def part(i):
            high, low = split(total[3, block(i, TILE), block(k, cols)])
            y_high[k, block(i, TILE), :] = high
            y_low[k, block(i, TILE), :] = low

        each(order // TILE, part)

    def split_rows(slot, first, count):
        def part(i):
            here = block(first * 4 + i, TILE // 4)
            high, low = split(total[slot, here, :])
            left_high[here, :] = high
            left_low[here, :] = low

        each(count * 4, part)

    def along_y(k, slot, first, count):
        split_rows(slot, first, count)

        def part(i):
            here = block(first + i, TILE)
            value = dot3((left_high[here, :], left_low[here, :]), (y_high[k], y_low[k])).T
            for j in range(TILE // own_rows):
                one = value[:, j * own_rows : (j + 1) * own_rows].reshape(peers, SUB, own_rows)
                stage[:, block(i * (TILE // own_rows) + j, SUB), :] = one

        each(count, part)

    def send_y(k, begin, length):
        here = block(begin, length)
        staged = stage.at[:, pl.ds(0, length), :]
        copy = pltpu.make_async_copy(staged, send_a.at[k, :, here, :], local_sem)
        own = pltpu.make_async_copy(stage.at[me, pl.ds(0, length), :], recv_a.at[k, me, here, :], own_sem)
        copy.start()
        own.start()
        copy.wait()
        own.wait()

        count = SPLIT if length == piece else 1

        def send(m):
            q = m % (peers - 1)
            to_day, to_row = peer(q)
            where = pl.ds(pl.multiple_of(begin * length + m // (peers - 1) * (length // count), SUB), length // count)
            pltpu.make_async_remote_copy(
                src_ref=send_a.at[k, to_day * rows + to_row, where, :],
                dst_ref=recv_a.at[k, me, where, :],
                send_sem=a_send.at[k],
                recv_sem=a_recv.at[k],
                device_id=(to_day, to_row),
                device_id_type=MESH,
            ).start()

        each(count * (peers - 1), send)

    prepare_y(0)

    def first(i):
        load_part(0, i).wait()
        along_y(0, 0, i, 1)
        send_y(0, i, fine)

    each(parts, first)
    load_field(1)

    def forward(m):
        n = m + 1
        k = n // steps

        @pl.when(n % steps == 0)
        def _():
            prepare_y(k)

        each(parts, lambda i: load_part(n, i).wait())

        @pl.when(n + 1 < chunks * steps)
        def _():
            load_field(n + 1)

        along_y(k, n % 2, 0, parts)
        send_y(k, n % steps, piece)

    each(chunks * steps - 1, forward)

    for load in loads:
        load.wait()
    load_x.wait()

    def turn_y(k):
        def part(i):
            high, low = split(total[3, block(i, TILE), block(k, cols)].T)
            yt_high[k, :, block(i, TILE)] = high
            yt_low[k, :, block(i, TILE)] = low

        each(order // TILE, part)

    each(chunks, turn_y)

    def turn_x(i):
        def part(j):
            value = total[2, block(i, TILE), block(j, TILE)]
            high, low = split(value)
            x_high[block(i, TILE), block(j, TILE)] = high
            x_low[block(i, TILE), block(j, TILE)] = low
            high, low = split(value.T)
            xt_high[block(j, TILE), block(i, TILE)] = high
            xt_low[block(j, TILE), block(i, TILE)] = low

        each(order // TILE, part)

    each(order // TILE, turn_x)
    day_high[...], day_low[...] = split(day_full[...])
    dayt_high[...], dayt_low[...] = split(day_full[...].T)
    day_col[...] = jnp.broadcast_to(eig_day[...], (total_days, total_days)).T

    def spread(i, j, value):
        for part in range(TILE // LANES):
            sheets[j * (TILE // LANES) + part, block(i, TILE), :] = value[:, part * LANES : (part + 1) * LANES]

    def settle(i, j, value):
        total[2, block(i, TILE), block(j, TILE)] = value

    def product(put, high, low):
        def part(n):
            i, j = n // (order // TILE), n % (order // TILE)
            left = left_high[block(i, TILE), :], left_low[block(i, TILE), :]
            put(i, j, dot3(left, (high[:, block(j, TILE)], low[:, block(j, TILE)])))

        each((height // TILE) * (order // TILE), part)

    def middle(k):
        rest = recv_a.at[k, pl.ds(0, peers - 1)]
        pltpu.make_async_copy(rest, rest, a_recv.at[k]).wait()

        def gather(n):
            pltpu.make_async_copy(
                recv_a.at[k, n], total.at[0, block(n // rows, depth), block(n % rows, own_rows)], local_sem
            ).start()

        each(peers, gather)
        pltpu.make_async_copy(total.at[0], total.at[0], local_sem).wait()
        split_rows(0, 0, parts)
        product(spread, x_high, x_low)

        def solve(j):
            shape = eig_x[:, block(j, LANES)]
            for b in range(SUB):
                where = (j, pl.ds(b, total_days, stride=SUB), slice(None))
                spectral = dot3((dayt_high[...], dayt_low[...]), split(sheets[where]))
                level = eig_y[k * cols + me * SUB + b]
                scaled = spectral / (day_col[...] * shape * level + noise[0])
                sheets[where] = dot3((day_high[...], day_low[...]), split(scaled))

        each(order // LANES, solve)

        def rejoin(n):
            i, j = n // (order // LANES), n % (order // LANES)
            high, low = split(sheets[j, block(i, TILE), :])
            left_high[block(i, TILE), block(j, LANES)] = high
            left_low[block(i, TILE), block(j, LANES)] = low

        each((height // TILE) * (order // LANES), rejoin)
        product(settle, xt_high, xt_low)

        def scatter(n):
            pltpu.make_async_copy(
                total.at[2, block(n // rows, depth), block(n % rows, own_rows)], send_b.at[k, n], local_sem
            ).start()

        each(peers, scatter)
        own = pltpu.make_async_copy(total.at[2, block(day, depth), block(row, own_rows)], recv_b.at[k, me], own_sem)
        own.start()
        pltpu.make_async_copy(total.at[2], total.at[2], local_sem).wait()
        own.wait()

        def send(q, here, arrived):
            to_day, to_row = peer(q)
            pltpu.make_async_remote_copy(
                src_ref=send_b.at[k, to_day * rows + to_row, here, :],
                dst_ref=recv_b.at[k, me, here, :],
                send_sem=b_send.at[k],
                recv_sem=arrived,
                device_id=(to_day, to_row),
                device_id_type=MESH,
            ).start()

        def send_part(n, first, count):
            tau, q = n // count, first + n % count
            send(q, block(tau, piece // SPLIT), b_recv.at[k, tau // SPLIT])

        def send_last(n, first, count):
            i, q = n // count, first + n % count
            send(q, block((steps - 1) * parts + i, fine), last_recv.at[i])

        @pl.when(k < chunks - 1)
        def _():
            each(steps * SPLIT * (peers - 1), lambda n: send_part(n, 0, peers - 1))

        @pl.when(k == chunks - 1)
        def _():
            far, near = peers // 2, peers - 1 - peers // 2
            each((steps - 1) * SPLIT * near, lambda n: send_part(n, far, near))
            each(parts * near, lambda n: send_last(n, far, near))
            each((steps - 1) * SPLIT * far, lambda n: send_part(n, 0, far))
            each(parts * far, lambda n: send_last(n, 0, far))

    each(chunks, middle)

    def clear(n):
        total[n // (height // TILE), block(n % (height // TILE), TILE), :] = jnp.zeros((TILE, order), jnp.float32)

    each(tiles * (height // TILE), clear)

    def along_b(k, tau, here, length, first, count, arrived):
        rest = recv_b.at[k, pl.ds(0, peers - 1), here, :]
        pltpu.make_async_copy(rest, rest, arrived).wait()
        load = pltpu.make_async_copy(recv_b.at[k, :, here, :], stage.at[:, pl.ds(0, length), :], local_sem)
        load.start()
        load.wait()

        def turn(i):
            high, low = split(stage[:, block(i, SUB), :].reshape(cols, own_rows).T)
            tall_high[block(i, own_rows), :] = high
            tall_low[block(i, own_rows), :] = low

        each(length // SUB, turn)

        def part(m):
            i, j = m // (order // TILE), m % (order // TILE)
            left = tall_high[block(i, TILE), :], tall_low[block(i, TILE), :]
            right = yt_high[k, :, block(j, TILE)], yt_low[k, :, block(j, TILE)]
            total[tau, block(first + i, TILE), block(j, TILE)] += dot3(left, right)

        each(count * (order // TILE), part)

    def backward(n):
        k, tau = n // steps, n % steps
        along_b(k, tau, block(tau, piece), piece, 0, parts, b_recv.at[k, tau])

    each(chunks * steps - 1, backward)

    def last(i):
        along_b(chunks - 1, steps - 1, block((steps - 1) * parts + i, fine), fine, i, 1, last_recv.at[i])

    each(parts, last)

    def drain(k):
        sent = send_a.at[k, pl.ds(0, peers - 1)]
        pltpu.make_async_copy(sent, sent, a_send.at[k]).wait()
        sent = send_b.at[k, pl.ds(0, peers - 1)]
        pltpu.make_async_copy(sent, sent, b_send.at[k]).wait()

    each(chunks, drain)


def fused(field, basis_day, basis_x, basis_y, eig_day, eig_x, eig_y, noise):
    own_days, own_rows, order = field.shape
    peers = lax.axis_size("day") * lax.axis_size("row")
    total_days = basis_day.shape[0]
    chunks = order // (peers * SUB)
    height = total_days * SUB
    span = height // own_rows
    steps = own_days // span
    depth = own_days * SUB
    f32, bf16 = jnp.float32, jnp.bfloat16
    wire = jax.ShapeDtypeStruct((chunks, peers, depth, own_rows), f32)
    anywhere = pl.BlockSpec(memory_space=pl.ANY)
    vmem = pl.BlockSpec(memory_space=pltpu.VMEM)
    cols = peers * SUB
    dma = pltpu.SemaphoreType.DMA
    square = pltpu.VMEM((order, order), bf16)
    small = pltpu.VMEM((total_days, total_days), bf16)
    result = pl.pallas_call(
        kernel,
        out_shape=(pltpu.VMEM((steps, height, order), f32), wire, wire, wire, wire),
        in_specs=[pl.BlockSpec(memory_space=pltpu.HBM)] * 8,
        out_specs=(vmem,) + (anywhere,) * 4,
        scratch_shapes=[
            pltpu.VMEM((chunks, order, cols), bf16),
            pltpu.VMEM((chunks, order, cols), bf16),
            pltpu.VMEM((chunks, cols, order), bf16),
            pltpu.VMEM((chunks, cols, order), bf16),
            square, square, square, square,
            small, small, small, small,
            pltpu.VMEM((total_days, total_days), f32),
            pltpu.VMEM((total_days, total_days), f32),
            pltpu.VMEM((1, total_days), f32),
            pltpu.VMEM((1, order), f32),
            pltpu.SMEM((order,), f32),
            pltpu.SMEM((1,), f32),
            pltpu.VMEM((order // LANES, height, LANES), f32),
            pltpu.VMEM((height, order), bf16),
            pltpu.VMEM((height, order), bf16),
            pltpu.VMEM((peers, span * SUB, own_rows), f32),
            pltpu.VMEM((height, cols), bf16),
            pltpu.VMEM((height, cols), bf16),
            dma((2, height // TILE)), dma((chunks,)), dma, dma((5,)), dma, dma,
            dma((chunks,)), dma((chunks,)), dma((chunks,)), dma((chunks, steps)), dma((height // TILE,)),
        ],
        compiler_params=pltpu.CompilerParams(
            collective_id=0, has_side_effects=True, vmem_limit_bytes=44 * 1024 * 1024
        ),
    )(
        field.reshape(own_days * own_rows, order), basis_day, basis_x, basis_y,
        eig_day.reshape(1, -1), eig_x.reshape(1, -1), eig_y, noise,
    )
    return result[0].reshape(field.shape)


def fits(field, basis_day, basis_x):
    own_days, own_rows, order = field.shape
    days, rows = lax.axis_size("day"), lax.axis_size("row")
    peers = days * rows
    height = basis_day.shape[0] * SUB
    return (
        days & (days - 1) == 0
        and rows & (rows - 1) == 0
        and own_rows == LANES
        and basis_day.shape[0] == LANES
        and order % (peers * SUB) == 0
        and peers * SUB == TILE
        and basis_x.shape[0] == order
        and height == order
        and own_days * own_rows == 4 * height
    )


def shift(block, axis, step):
    size = lax.axis_size(axis)
    if step % size == 0:
        return block
    return lax.ppermute(block, axis, [(i, (i + step) % size) for i in range(size)])


def rolled(array, dim, blocks, first, sign):
    width = array.shape[dim] // blocks
    starts = [((first + sign * j) % blocks) * width for j in range(blocks)]
    return jnp.concatenate([lax.dynamic_slice_in_dim(array, start, width, dim) for start in starts], axis=dim)


def exchanged(field, basis_day, basis_x, basis_y, eig_day, eig_x, eig_y, noise):
    precise = lax.Precision.HIGH
    days = lax.axis_size("day")
    rows = lax.axis_size("row")
    day = lax.axis_index("day")
    row = lax.axis_index("row")
    local_days, local_rows, grid_cols = field.shape
    grid_rows = basis_x.shape[0]
    own_cols = grid_cols // rows
    own_spec = grid_rows // days
    chunks = max(1, min(CHUNKS, own_cols // 32))
    width = own_cols // chunks

    def product(spec, left, right):
        return jnp.einsum(spec, left, right, precision=precise, preferred_element_type=jnp.float32)

    turn_x = rolled(rolled(basis_x, 0, rows, row, -1), 1, days, day, 1)
    turn_y = rolled(basis_y.T, 0, rows, row, 1).reshape(rows, chunks, width, grid_cols)
    turn_day = rolled(basis_day, 0, days, day, -1)
    part_x = lax.dynamic_slice_in_dim(eig_x, day * own_spec, own_spec)
    part_y = lax.dynamic_slice_in_dim(eig_y, row * own_cols, own_cols)
    parts = []
    for chunk in range(chunks):
        basis = turn_y[:, chunk].reshape(rows * width, grid_cols)
        along_y = product("by,txy->btx", basis, field)
        got = [shift(along_y[j * width : (j + 1) * width], "row", j) for j in range(rows)]
        along_x = product("btx,xa->bta", jnp.concatenate(got, axis=2), turn_x)
        got = [shift(along_x[:, :, j * own_spec : (j + 1) * own_spec], "day", j) for j in range(days)]
        spectral = product("ts,bta->bsa", turn_day, jnp.concatenate(got, axis=1))
        own_y = part_y[chunk * width : (chunk + 1) * width]
        spectrum = eig_day[None, :, None] * part_x[None, None, :] * own_y[:, None, None] + noise[0]
        back_day = product("ts,bsa->bta", turn_day, spectral / spectrum)
        got = [shift(back_day[:, j * local_days : (j + 1) * local_days], "day", -j) for j in range(days)]
        back_x = product("bta,xa->btx", jnp.concatenate(got, axis=2), turn_x)
        got = [shift(back_x[:, :, j * local_rows : (j + 1) * local_rows], "row", -j) for j in range(rows)]
        parts.append((basis, jnp.concatenate(got, axis=0)))
    weights = None
    for group in (parts[:-1], parts[-1:]):
        if group:
            basis = jnp.concatenate([g[0] for g in group], axis=0)
            value = product("btx,by->txy", jnp.concatenate([g[1] for g in group], axis=0), basis)
            weights = value if weights is None else weights + value
    return weights


def body(field, basis_day, basis_x, *rest):
    route = fused if fits(field, basis_day, basis_x) else exchanged
    return route(field, basis_day, basis_x, *rest)


def solution(mesh):
    in_specs = (P("day", "row", None), P(), P(), P(), P(), P(), P(), P())
    out_specs = P("day", "row", None)
    return jax.shard_map(body, mesh=mesh, in_specs=in_specs, out_specs=out_specs, check_vma=False)
```

```python
import functools
import jax
import jax.numpy as jnp
from jax import lax
from jax.experimental import pallas as pl
from jax.experimental.pallas import tpu as pltpu
from jax.sharding import PartitionSpec as P

CHUNKS = 4
SUB = 8
LANES = 128
TILE = 256
SPLIT = 2
MESH = pl.DeviceIdType.MESH


def split(value):
    high = value.astype(jnp.bfloat16)
    low = (value - high.astype(jnp.float32)).astype(jnp.bfloat16)
    return high, low


def dot3(left, right):
    def one(a, b):
        return jnp.dot(a, b, preferred_element_type=jnp.float32)

    return one(left[0], right[0]) + (one(left[0], right[1]) + one(left[1], right[0]))


def flipped(index, mask, size):
    total, bit = 0, 1
    while bit < size:
        total = total + bit * ((index // bit + mask // bit) % 2)
        bit *= 2
    return total


def block(start, size):
    return pl.ds(pl.multiple_of(start * size, size), size)


def each(count, fn):
    def step(i, carry):
        fn(i)
        return carry

    lax.fori_loop(0, count, step, 0)


def kernel(
    field, basis_day, basis_x, basis_y, day_values, x_values, y_values, noise_value,
    total, tail, last_high, last_low, send_a, recv_a, send_b, recv_b,
    y_high, y_low, yt_high, yt_low, x_high, x_low, xt_high, xt_low,
    day_high, day_low, dayt_high, dayt_low, day_col, day_full, eig_day, eig_x, eig_y, noise,
    sheets, left_high, left_low, stage, tall_high, tall_low,
    load_sem, y_sem, x_sem, small_sem, local_sem, own_sem, tail_sem,
    a_send, a_recv, b_send, b_recv, last_recv,
):
    days = lax.axis_size("day")
    rows = lax.axis_size("row")
    day = lax.axis_index("day")
    row = lax.axis_index("row")
    peers = days * rows
    me = day * rows + row
    chunks, _, depth, own_rows = recv_a.shape
    cols = peers * SUB
    tiles, height, order = total.shape[0], total.shape[1], total.shape[2]
    span = height // own_rows
    steps = depth // (span * SUB)
    piece = span * SUB
    total_days = basis_day.shape[0]

    barrier = pltpu.get_barrier_semaphore()

    def peer(q):
        half = peers // 2
        near = q // half
        mask = (1 - near) * (half + q) + near * (peers - 1 - q)
        i, j = mask // days, mask % days
        to_row = flipped(row, i, rows)
        to_day = flipped(day, j, days)
        return to_day, to_row

    def greet(q):
        pl.semaphore_signal(barrier, inc=1, device_id=peer(q), device_id_type=MESH)

    parts = height // TILE
    fine = piece // parts

    def load_part(n, i):
        source = field.at[block((n % steps) * parts + i, TILE)]
        return pltpu.make_async_copy(source, total.at[n % 2, block(i, TILE)], load_sem.at[n % 2, i])

    def load_field(n):
        each(parts, lambda i: load_part(n, i).start())

    def load_y(k):
        return pltpu.make_async_copy(basis_y.at[:, block(k, cols)], total.at[3, :, block(k, cols)], y_sem.at[k])

    load_y(0).start()
    load_field(0)
    each(peers - 1, greet)
    each(chunks - 1, lambda k: load_y(k + 1).start())
    load_x = pltpu.make_async_copy(basis_x, total.at[2], x_sem)
    load_x.start()
    loads = [
        pltpu.make_async_copy(source, target, small_sem.at[i])
        for i, (source, target) in enumerate(
            ((basis_day, day_full), (day_values, eig_day), (x_values, eig_x), (y_values, eig_y), (noise_value, noise))
        )
    ]
    for load in loads:
        load.start()
    pl.semaphore_wait(barrier, peers - 1)

    def prepare_y(k):
        load_y(k).wait()

        def part(i):
            high, low = split(total[3, block(i, TILE), block(k, cols)])
            y_high[k, block(i, TILE), :] = high
            y_low[k, block(i, TILE), :] = low

        each(order // TILE, part)

    def split_rows(slot, first, count):
        def part(i):
            here = block(first * 4 + i, TILE // 4)
            high, low = split(total[slot, here, :])
            left_high[here, :] = high
            left_low[here, :] = low

        each(count * 4, part)

    def along_y(k, slot, first, count):
        split_rows(slot, first, count)

        def part(i):
            here = block(first + i, TILE)
            value = dot3((left_high[here, :], left_low[here, :]), (y_high[k], y_low[k])).T
            for j in range(TILE // own_rows):
                one = value[:, j * own_rows : (j + 1) * own_rows].reshape(peers, SUB, own_rows)
                stage[:, block(i * (TILE // own_rows) + j, SUB), :] = one

        each(count, part)

    def send_y(k, begin, length):
        here = block(begin, length)
        staged = stage.at[:, pl.ds(0, length), :]
        copy = pltpu.make_async_copy(staged, send_a.at[k, :, here, :], local_sem)
        own = pltpu.make_async_copy(stage.at[me, pl.ds(0, length), :], recv_a.at[k, me, here, :], own_sem)
        copy.start()
        own.start()
        copy.wait()
        own.wait()

        count = SPLIT if length == piece else 1

        def send(m):
            q = m % (peers - 1)
            to_day, to_row = peer(q)
            where = pl.ds(pl.multiple_of(begin * length + m // (peers - 1) * (length // count), SUB), length // count)
            pltpu.make_async_remote_copy(
                src_ref=send_a.at[k, to_day * rows + to_row, where, :],
                dst_ref=recv_a.at[k, me, where, :],
                send_sem=a_send.at[k],
                recv_sem=a_recv.at[k],
                device_id=(to_day, to_row),
                device_id_type=MESH,
            ).start()

        each(count * (peers - 1), send)

    prepare_y(0)

    def first(i):
        load_part(0, i).wait()
        along_y(0, 0, i, 1)
        send_y(0, i, fine)

    each(parts, first)
    load_field(1)

    def forward(m):
        n = m + 1
        k = n // steps

        @pl.when(n % steps == 0)
        def _():
            prepare_y(k)

        each(parts, lambda i: load_part(n, i).wait())

        @pl.when(n + 1 < chunks * steps)
        def _():
            load_field(n + 1)

        along_y(k, n % 2, 0, parts)
        send_y(k, n % steps, piece)

    each(chunks * steps - 1, forward)

    for load in loads:
        load.wait()
    load_x.wait()

    def turn_y(k):
        def part(i):
            high, low = split(total[3, block(i, TILE), block(k, cols)].T)
            yt_high[k, :, block(i, TILE)] = high
            yt_low[k, :, block(i, TILE)] = low

        each(order // TILE, part)

    each(chunks, turn_y)

    def turn_x(i):
        def part(j):
            value = total[2, block(i, TILE), block(j, TILE)]
            high, low = split(value)
            x_high[block(i, TILE), block(j, TILE)] = high
            x_low[block(i, TILE), block(j, TILE)] = low
            high, low = split(value.T)
            xt_high[block(j, TILE), block(i, TILE)] = high
            xt_low[block(j, TILE), block(i, TILE)] = low

        each(order // TILE, part)

    each(order // TILE, turn_x)
    last_high[...] = yt_high[chunks - 1]
    last_low[...] = yt_low[chunks - 1]
    day_high[...], day_low[...] = split(day_full[...])
    dayt_high[...], dayt_low[...] = split(day_full[...].T)
    day_col[...] = jnp.broadcast_to(eig_day[...], (total_days, total_days)).T

    def spread(i, j, value):
        for part in range(TILE // LANES):
            sheets[j * (TILE // LANES) + part, block(i, TILE), :] = value[:, part * LANES : (part + 1) * LANES]

    def settle(i, j, value):
        total[2, block(i, TILE), block(j, TILE)] = value

    def product(put, high, low):
        def part(n):
            i, j = n // (order // TILE), n % (order // TILE)
            left = left_high[block(i, TILE), :], left_low[block(i, TILE), :]
            put(i, j, dot3(left, (high[:, block(j, TILE)], low[:, block(j, TILE)])))

        each((height // TILE) * (order // TILE), part)

    def middle(k):
        rest = recv_a.at[k, pl.ds(0, peers - 1)]
        pltpu.make_async_copy(rest, rest, a_recv.at[k]).wait()

        def gather(n):
            pltpu.make_async_copy(
                recv_a.at[k, n], total.at[0, block(n // rows, depth), block(n % rows, own_rows)], local_sem
            ).start()

        each(peers, gather)
        pltpu.make_async_copy(total.at[0], total.at[0], local_sem).wait()
        split_rows(0, 0, parts)
        product(spread, x_high, x_low)

        def solve(j):
            shape = eig_x[:, block(j, LANES)]
            for b in range(SUB):
                where = (j, pl.ds(b, total_days, stride=SUB), slice(None))
                spectral = dot3((dayt_high[...], dayt_low[...]), split(sheets[where]))
                level = eig_y[k * cols + me * SUB + b]
                scaled = spectral / (day_col[...] * shape * level + noise[0])
                sheets[where] = dot3((day_high[...], day_low[...]), split(scaled))

        each(order // LANES, solve)

        def rejoin(n):
            i, j = n // (order // LANES), n % (order // LANES)
            high, low = split(sheets[j, block(i, TILE), :])
            left_high[block(i, TILE), block(j, LANES)] = high
            left_low[block(i, TILE), block(j, LANES)] = low

        each((height // TILE) * (order // LANES), rejoin)
        product(settle, xt_high, xt_low)

        def scatter(n):
            pltpu.make_async_copy(
                total.at[2, block(n // rows, depth), block(n % rows, own_rows)], send_b.at[k, n], local_sem
            ).start()

        each(peers, scatter)
        own = pltpu.make_async_copy(total.at[2, block(day, depth), block(row, own_rows)], recv_b.at[k, me], own_sem)
        own.start()

        @pl.when(k == chunks - 1)
        def _():
            source = total.at[2, block((day + 1) * steps * parts - 1, fine), block(row, own_rows)]
            copy = pltpu.make_async_copy(source, tail.at[me], tail_sem)
            copy.start()
            copy.wait()

        pltpu.make_async_copy(total.at[2], total.at[2], local_sem).wait()
        own.wait()

        def send(q, here, target, arrived):
            to_day, to_row = peer(q)
            pltpu.make_async_remote_copy(
                src_ref=send_b.at[k, to_day * rows + to_row, here, :],
                dst_ref=target,
                send_sem=b_send.at[k],
                recv_sem=arrived,
                device_id=(to_day, to_row),
                device_id_type=MESH,
            ).start()

        def send_part(n, first, count):
            tau, q = n // count, first + n % count
            here = block(tau, piece // SPLIT)
            send(q, here, recv_b.at[k, me, here, :], b_recv.at[k, tau // SPLIT])

        def send_last(n, first, count):
            i, q = n // count, first + n % count
            here = block((steps - 1) * parts + i, fine)
            send(q, here, recv_b.at[k, me, here, :], last_recv.at[i])

        def send_tail(q):
            send(q, block(steps * parts - 1, fine), tail.at[me], last_recv.at[parts - 1])

        @pl.when(k < chunks - 1)
        def _():
            each(steps * SPLIT * (peers - 1), lambda n: send_part(n, 0, peers - 1))

        @pl.when(k == chunks - 1)
        def _():
            far, near = peers // 2, peers - 1 - peers // 2
            each((steps - 1) * SPLIT * near, lambda n: send_part(n, far, near))
            each((parts - 1) * near, lambda n: send_last(n, far, near))
            each(near, lambda n: send_tail(far + n))
            each((steps - 1) * SPLIT * far, lambda n: send_part(n, 0, far))
            each((parts - 1) * far, lambda n: send_last(n, 0, far))
            each(far, send_tail)

    each(chunks, middle)

    def clear(n):
        total[n // (height // TILE), block(n % (height // TILE), TILE), :] = jnp.zeros((TILE, order), jnp.float32)

    each(tiles * (height // TILE), clear)

    def along_b(k, tau, here, length, first, count, arrived):
        rest = recv_b.at[k, pl.ds(0, peers - 1), here, :]
        pltpu.make_async_copy(rest, rest, arrived).wait()
        load = pltpu.make_async_copy(recv_b.at[k, :, here, :], stage.at[:, pl.ds(0, length), :], local_sem)
        load.start()
        load.wait()

        def turn(i):
            high, low = split(stage[:, block(i, SUB), :].reshape(cols, own_rows).T)
            tall_high[block(i, own_rows), :] = high
            tall_low[block(i, own_rows), :] = low

        each(length // SUB, turn)

        def part(m):
            i, j = m // (order // TILE), m % (order // TILE)
            left = tall_high[block(i, TILE), :], tall_low[block(i, TILE), :]
            right = yt_high[k, :, block(j, TILE)], yt_low[k, :, block(j, TILE)]
            total[tau, block(first + i, TILE), block(j, TILE)] += dot3(left, right)

        each(count * (order // TILE), part)

    def backward(n):
        k, tau = n // steps, n % steps
        along_b(k, tau, block(tau, piece), piece, 0, parts, b_recv.at[k, tau])

    each(chunks * steps - 1, backward)

    def last(i):
        along_b(chunks - 1, steps - 1, block((steps - 1) * parts + i, fine), fine, i, 1, last_recv.at[i])

    each(parts - 1, last)
    rest = tail.at[pl.ds(0, peers - 1)]
    pltpu.make_async_copy(rest, rest, last_recv.at[parts - 1]).wait()

    def drain(k):
        sent = send_a.at[k, pl.ds(0, peers - 1)]
        pltpu.make_async_copy(sent, sent, a_send.at[k]).wait()
        sent = send_b.at[k, pl.ds(0, peers - 1)]
        pltpu.make_async_copy(sent, sent, b_send.at[k]).wait()

    each(chunks, drain)


def closing(total, tail, right_high, right_low, out, left_high, left_low, final, sems):
    steps, height, order = total.shape
    peers, fine, own_rows = tail.shape
    done = height - TILE
    copies = [
        pltpu.make_async_copy(total.at[tau], out.at[pl.ds(tau * height, height)], sems.at[tau])
        for tau in range(steps - 1)
    ]
    first = (steps - 1) * height
    copies.append(pltpu.make_async_copy(total.at[steps - 1, pl.ds(0, done)], out.at[pl.ds(first, done)], sems.at[steps - 1]))
    for copy in copies:
        copy.start()
    for i in range(fine // SUB):
        high, low = split(tail[:, i * SUB : (i + 1) * SUB, :].reshape(peers * SUB, own_rows).T)
        left_high[i * own_rows : (i + 1) * own_rows, :] = high
        left_low[i * own_rows : (i + 1) * own_rows, :] = low

    def part(j):
        here = block(j, TILE)
        value = dot3((left_high[...], left_low[...]), (right_high[:, here], right_low[:, here]))
        final[:, here] = total[steps - 1, pl.ds(done, TILE), here] + value

    each(order // TILE, part)
    copies.append(pltpu.make_async_copy(final, out.at[pl.ds(first + done, TILE)], sems.at[steps]))
    copies[-1].start()
    for copy in copies:
        copy.wait()


def fused(field, basis_day, basis_x, basis_y, eig_day, eig_x, eig_y, noise):
    own_days, own_rows, order = field.shape
    peers = lax.axis_size("day") * lax.axis_size("row")
    total_days = basis_day.shape[0]
    chunks = order // (peers * SUB)
    height = total_days * SUB
    span = height // own_rows
    steps = own_days // span
    depth = own_days * SUB
    f32, bf16 = jnp.float32, jnp.bfloat16
    wire = jax.ShapeDtypeStruct((chunks, peers, depth, own_rows), f32)
    anywhere = pl.BlockSpec(memory_space=pl.ANY)
    vmem = pl.BlockSpec(memory_space=pltpu.VMEM)
    cols = peers * SUB
    dma = pltpu.SemaphoreType.DMA
    square = pltpu.VMEM((order, order), bf16)
    small = pltpu.VMEM((total_days, total_days), bf16)
    result = pl.pallas_call(
        kernel,
        out_shape=(
            pltpu.VMEM((steps, height, order), f32),
            pltpu.VMEM((peers, TILE // own_rows * SUB, own_rows), f32),
            pltpu.VMEM((cols, order), bf16),
            pltpu.VMEM((cols, order), bf16),
            wire, wire, wire, wire,
        ),
        in_specs=[pl.BlockSpec(memory_space=pltpu.HBM)] * 8,
        out_specs=(vmem,) * 4 + (anywhere,) * 4,
        scratch_shapes=[
            pltpu.VMEM((chunks, order, cols), bf16),
            pltpu.VMEM((chunks, order, cols), bf16),
            pltpu.VMEM((chunks, cols, order), bf16),
            pltpu.VMEM((chunks, cols, order), bf16),
            square, square, square, square,
            small, small, small, small,
            pltpu.VMEM((total_days, total_days), f32),
            pltpu.VMEM((total_days, total_days), f32),
            pltpu.VMEM((1, total_days), f32),
            pltpu.VMEM((1, order), f32),
            pltpu.SMEM((order,), f32),
            pltpu.SMEM((1,), f32),
            pltpu.VMEM((order // LANES, height, LANES), f32),
            pltpu.VMEM((height, order), bf16),
            pltpu.VMEM((height, order), bf16),
            pltpu.VMEM((peers, span * SUB, own_rows), f32),
            pltpu.VMEM((height, cols), bf16),
            pltpu.VMEM((height, cols), bf16),
            dma((2, height // TILE)), dma((chunks,)), dma, dma((5,)), dma, dma, dma,
            dma((chunks,)), dma((chunks,)), dma((chunks,)), dma((chunks, steps)), dma((height // TILE,)),
        ],
        compiler_params=pltpu.CompilerParams(
            collective_id=0, has_side_effects=True, vmem_limit_bytes=44 * 1024 * 1024
        ),
    )(
        field.reshape(own_days * own_rows, order), basis_day, basis_x, basis_y,
        eig_day.reshape(1, -1), eig_x.reshape(1, -1), eig_y, noise,
    )
    return pl.pallas_call(
        closing,
        out_shape=jax.ShapeDtypeStruct((own_days * own_rows, order), f32),
        in_specs=[vmem] * 4,
        out_specs=anywhere,
        scratch_shapes=[
            pltpu.VMEM((TILE, cols), bf16),
            pltpu.VMEM((TILE, cols), bf16),
            pltpu.VMEM((TILE, order), f32),
            dma((steps + 1,)),
        ],
        compiler_params=pltpu.CompilerParams(vmem_limit_bytes=16 * 1024 * 1024),
    )(*result[:4]).reshape(field.shape)


def fits(field, basis_day, basis_x):
    own_days, own_rows, order = field.shape
    days, rows = lax.axis_size("day"), lax.axis_size("row")
    peers = days * rows
    height = basis_day.shape[0] * SUB
    return (
        days & (days - 1) == 0
        and rows & (rows - 1) == 0
        and own_rows == LANES
        and basis_day.shape[0] == LANES
        and order % (peers * SUB) == 0
        and peers * SUB == TILE
        and basis_x.shape[0] == order
        and height == order
        and own_days * own_rows == 4 * height
    )


def shift(block, axis, step):
    size = lax.axis_size(axis)
    if step % size == 0:
        return block
    return lax.ppermute(block, axis, [(i, (i + step) % size) for i in range(size)])


def rolled(array, dim, blocks, first, sign):
    width = array.shape[dim] // blocks
    starts = [((first + sign * j) % blocks) * width for j in range(blocks)]
    return jnp.concatenate([lax.dynamic_slice_in_dim(array, start, width, dim) for start in starts], axis=dim)


def exchanged(field, basis_day, basis_x, basis_y, eig_day, eig_x, eig_y, noise):
    precise = lax.Precision.HIGH
    days = lax.axis_size("day")
    rows = lax.axis_size("row")
    day = lax.axis_index("day")
    row = lax.axis_index("row")
    local_days, local_rows, grid_cols = field.shape
    grid_rows = basis_x.shape[0]
    own_cols = grid_cols // rows
    own_spec = grid_rows // days
    chunks = max(1, min(CHUNKS, own_cols // 32))
    width = own_cols // chunks

    def product(spec, left, right):
        return jnp.einsum(spec, left, right, precision=precise, preferred_element_type=jnp.float32)

    turn_x = rolled(rolled(basis_x, 0, rows, row, -1), 1, days, day, 1)
    turn_y = rolled(basis_y.T, 0, rows, row, 1).reshape(rows, chunks, width, grid_cols)
    turn_day = rolled(basis_day, 0, days, day, -1)
    part_x = lax.dynamic_slice_in_dim(eig_x, day * own_spec, own_spec)
    part_y = lax.dynamic_slice_in_dim(eig_y, row * own_cols, own_cols)
    parts = []
    for chunk in range(chunks):
        basis = turn_y[:, chunk].reshape(rows * width, grid_cols)
        along_y = product("by,txy->btx", basis, field)
        got = [shift(along_y[j * width : (j + 1) * width], "row", j) for j in range(rows)]
        along_x = product("btx,xa->bta", jnp.concatenate(got, axis=2), turn_x)
        got = [shift(along_x[:, :, j * own_spec : (j + 1) * own_spec], "day", j) for j in range(days)]
        spectral = product("ts,bta->bsa", turn_day, jnp.concatenate(got, axis=1))
        own_y = part_y[chunk * width : (chunk + 1) * width]
        spectrum = eig_day[None, :, None] * part_x[None, None, :] * own_y[:, None, None] + noise[0]
        back_day = product("ts,bsa->bta", turn_day, spectral / spectrum)
        got = [shift(back_day[:, j * local_days : (j + 1) * local_days], "day", -j) for j in range(days)]
        back_x = product("bta,xa->btx", jnp.concatenate(got, axis=2), turn_x)
        got = [shift(back_x[:, :, j * local_rows : (j + 1) * local_rows], "row", -j) for j in range(rows)]
        parts.append((basis, jnp.concatenate(got, axis=0)))
    weights = None
    for group in (parts[:-1], parts[-1:]):
        if group:
            basis = jnp.concatenate([g[0] for g in group], axis=0)
            value = product("btx,by->txy", jnp.concatenate([g[1] for g in group], axis=0), basis)
            weights = value if weights is None else weights + value
    return weights


def body(field, basis_day, basis_x, *rest):
    route = fused if fits(field, basis_day, basis_x) else exchanged
    return route(field, basis_day, basis_x, *rest)


def solution(mesh):
    in_specs = (P("day", "row", None), P(), P(), P(), P(), P(), P(), P())
    out_specs = P("day", "row", None)
    return jax.shard_map(body, mesh=mesh, in_specs=in_specs, out_specs=out_specs, check_vma=False)
```

```python
import functools
import jax
import jax.numpy as jnp
from jax import lax
from jax.experimental import pallas as pl
from jax.experimental.pallas import tpu as pltpu
from jax.sharding import PartitionSpec as P

CHUNKS = 4
SUB = 8
LANES = 128
TILE = 256
SPLIT = 2
MESH = pl.DeviceIdType.MESH


def split(value):
    high = value.astype(jnp.bfloat16)
    low = (value - high.astype(jnp.float32)).astype(jnp.bfloat16)
    return high, low


def dot3(left, right):
    def one(a, b):
        return jnp.dot(a, b, preferred_element_type=jnp.float32)

    return one(left[0], right[0]) + (one(left[0], right[1]) + one(left[1], right[0]))


def turns(index, size):
    return [bit * (1 - 2 * (index // bit % 2)) for bit in (1 << n for n in range(size.bit_length() - 1))]


def flipped(index, steps, mask):
    return index + sum((mask // (1 << n)) % 2 * step for n, step in enumerate(steps))


def block(start, size):
    return pl.ds(pl.multiple_of(start * size, size), size)


def each(count, fn):
    def step(i, carry):
        fn(i)
        return carry

    lax.fori_loop(0, count, step, 0)


def kernel(
    field, basis_day, basis_x, basis_y, day_values, x_values, y_values, noise_value,
    total, tail, last_high, last_low, send_a, recv_a, send_b, recv_b,
    y_high, y_low, yt_high, yt_low, x_high, x_low, xt_high, xt_low,
    day_high, day_low, dayt_high, dayt_low, day_col, day_full, eig_day, eig_x, eig_y, noise,
    sheets, left_high, left_low, stage, tall_high, tall_low,
    load_sem, y_sem, x_sem, small_sem, local_sem, own_sem, tail_sem,
    a_send, a_recv, b_send, b_recv, last_recv,
):
    days = lax.axis_size("day")
    rows = lax.axis_size("row")
    day = lax.axis_index("day")
    row = lax.axis_index("row")
    peers = days * rows
    me = day * rows + row
    chunks, _, depth, own_rows = recv_a.shape
    cols = peers * SUB
    tiles, height, order = total.shape[0], total.shape[1], total.shape[2]
    span = height // own_rows
    steps = depth // (span * SUB)
    piece = span * SUB
    total_days = basis_day.shape[0]

    day_turns, row_turns = turns(day, days), turns(row, rows)
    barrier = pltpu.get_barrier_semaphore()

    def peer(q):
        half = peers // 2
        near = q // half
        mask = (1 - near) * (half + q) + near * (peers - 1 - q)
        i, j = mask // days, mask % days
        return flipped(day, day_turns, j), flipped(row, row_turns, i)

    def greet():
        for mask in range(peers - 1, 0, -1):
            other = flipped(day, day_turns, mask % days), flipped(row, row_turns, mask // days)
            pl.semaphore_signal(barrier, inc=1, device_id=other, device_id_type=MESH)

    parts = height // TILE
    fine = piece // parts

    def load_part(n, i):
        source = field.at[block((n % steps) * parts + i, TILE)]
        return pltpu.make_async_copy(source, total.at[n % 2, block(i, TILE)], load_sem.at[n % 2, i])

    def load_field(n):
        each(parts, lambda i: load_part(n, i).start())

    def load_y(k):
        return pltpu.make_async_copy(basis_y.at[:, block(k, cols)], total.at[3, :, block(k, cols)], y_sem.at[k])

    load_y(0).start()
    load_part(0, 0).start()
    greet()
    load_x = pltpu.make_async_copy(basis_x, total.at[2], x_sem)
    loads = [
        pltpu.make_async_copy(source, target, small_sem.at[i])
        for i, (source, target) in enumerate(
            ((basis_day, day_full), (day_values, eig_day), (x_values, eig_x), (y_values, eig_y), (noise_value, noise))
        )
    ]

    def prepare_y(k):
        load_y(k).wait()

        def part(i):
            high, low = split(total[3, block(i, TILE), block(k, cols)])
            y_high[k, block(i, TILE), :] = high
            y_low[k, block(i, TILE), :] = low

        each(order // TILE, part)

    def split_rows(slot, first, count):
        def part(i):
            here = block(first * 4 + i, TILE // 4)
            high, low = split(total[slot, here, :])
            left_high[here, :] = high
            left_low[here, :] = low

        each(count * 4, part)

    def along_y(k, slot, first, count):
        split_rows(slot, first, count)

        def part(i):
            here = block(first + i, TILE)
            value = dot3((left_high[here, :], left_low[here, :]), (y_high[k], y_low[k])).T
            for j in range(TILE // own_rows):
                one = value[:, j * own_rows : (j + 1) * own_rows].reshape(peers, SUB, own_rows)
                stage[:, block(i * (TILE // own_rows) + j, SUB), :] = one

        each(count, part)

    def send_y(k, begin, length):
        here = block(begin, length)
        staged = stage.at[:, pl.ds(0, length), :]
        copy = pltpu.make_async_copy(staged, send_a.at[k, :, here, :], local_sem)
        own = pltpu.make_async_copy(stage.at[me, pl.ds(0, length), :], recv_a.at[k, me, here, :], own_sem)
        copy.start()
        own.start()
        copy.wait()
        count = SPLIT if length == piece else 1

        def send(m):
            q = m % (peers - 1)
            to_day, to_row = peer(q)
            where = pl.ds(pl.multiple_of(begin * length + m // (peers - 1) * (length // count), SUB), length // count)
            pltpu.make_async_remote_copy(
                src_ref=send_a.at[k, to_day * rows + to_row, where, :],
                dst_ref=recv_a.at[k, me, where, :],
                send_sem=a_send.at[k],
                recv_sem=a_recv.at[k],
                device_id=(to_day, to_row),
                device_id_type=MESH,
            ).start()

        each(count * (peers - 1), send)
        own.wait()

    prepare_y(0)
    load_part(0, 0).wait()
    each(parts - 1, lambda i: load_part(0, i + 1).start())
    along_y(0, 0, 0, 1)
    pl.semaphore_wait(barrier, peers - 1)
    send_y(0, 0, fine)
    load_field(1)
    each(chunks - 1, lambda k: load_y(k + 1).start())

    def first(i):
        load_part(0, i + 1).wait()
        along_y(0, 0, i + 1, 1)
        send_y(0, i + 1, fine)

    each(parts - 1, first)
    load_x.start()
    for load in loads:
        load.start()

    def forward(m):
        n = m + 1
        k = n // steps

        @pl.when(n % steps == 0)
        def _():
            prepare_y(k)

        each(parts, lambda i: load_part(n, i).wait())

        @pl.when(n + 1 < chunks * steps)
        def _():
            load_field(n + 1)

        along_y(k, n % 2, 0, parts)
        send_y(k, n % steps, piece)

    each(chunks * steps - 1, forward)

    for load in loads:
        load.wait()
    load_x.wait()

    def turn_y(k):
        def part(i):
            high, low = split(total[3, block(i, TILE), block(k, cols)].T)
            yt_high[k, :, block(i, TILE)] = high
            yt_low[k, :, block(i, TILE)] = low

        each(order // TILE, part)

    each(chunks, turn_y)

    def turn_x(i):
        def part(j):
            value = total[2, block(i, TILE), block(j, TILE)]
            high, low = split(value)
            x_high[block(i, TILE), block(j, TILE)] = high
            x_low[block(i, TILE), block(j, TILE)] = low
            high, low = split(value.T)
            xt_high[block(j, TILE), block(i, TILE)] = high
            xt_low[block(j, TILE), block(i, TILE)] = low

        each(order // TILE, part)

    each(order // TILE, turn_x)
    last_high[...] = yt_high[chunks - 1]
    last_low[...] = yt_low[chunks - 1]
    day_high[...], day_low[...] = split(day_full[...])
    dayt_high[...], dayt_low[...] = split(day_full[...].T)
    day_col[...] = jnp.broadcast_to(eig_day[...], (total_days, total_days)).T

    def spread(i, j, value):
        for part in range(TILE // LANES):
            sheets[j * (TILE // LANES) + part, block(i, TILE), :] = value[:, part * LANES : (part + 1) * LANES]

    def settle(i, j, value):
        total[2, block(i, TILE), block(j, TILE)] = value

    def product(put, high, low):
        def part(n):
            i, j = n // (order // TILE), n % (order // TILE)
            left = left_high[block(i, TILE), :], left_low[block(i, TILE), :]
            put(i, j, dot3(left, (high[:, block(j, TILE)], low[:, block(j, TILE)])))

        each((height // TILE) * (order // TILE), part)

    def middle(k):
        rest = recv_a.at[k, pl.ds(0, peers - 1)]
        pltpu.make_async_copy(rest, rest, a_recv.at[k]).wait()

        def gather(n):
            pltpu.make_async_copy(
                recv_a.at[k, n], total.at[0, block(n // rows, depth), block(n % rows, own_rows)], local_sem
            ).start()

        each(peers, gather)
        pltpu.make_async_copy(total.at[0], total.at[0], local_sem).wait()
        split_rows(0, 0, parts)
        product(spread, x_high, x_low)

        def solve(j):
            shape = eig_x[:, block(j, LANES)]
            for b in range(SUB):
                where = (j, pl.ds(b, total_days, stride=SUB), slice(None))
                spectral = dot3((dayt_high[...], dayt_low[...]), split(sheets[where]))
                level = eig_y[k * cols + me * SUB + b]
                scaled = spectral / (day_col[...] * shape * level + noise[0])
                sheets[where] = dot3((day_high[...], day_low[...]), split(scaled))

        each(order // LANES, solve)

        def rejoin(n):
            i, j = n // (order // LANES), n % (order // LANES)
            high, low = split(sheets[j, block(i, TILE), :])
            left_high[block(i, TILE), block(j, LANES)] = high
            left_low[block(i, TILE), block(j, LANES)] = low

        each((height // TILE) * (order // LANES), rejoin)
        product(settle, xt_high, xt_low)

        def scatter(n):
            pltpu.make_async_copy(
                total.at[2, block(n // rows, depth), block(n % rows, own_rows)], send_b.at[k, n], local_sem
            ).start()

        each(peers, scatter)
        own = pltpu.make_async_copy(total.at[2, block(day, depth), block(row, own_rows)], recv_b.at[k, me], own_sem)
        own.start()

        @pl.when(k == chunks - 1)
        def _():
            source = total.at[2, block((day + 1) * steps * parts - 1, fine), block(row, own_rows)]
            copy = pltpu.make_async_copy(source, tail.at[me], tail_sem)
            copy.start()
            copy.wait()

        pltpu.make_async_copy(total.at[2], total.at[2], local_sem).wait()
        own.wait()

        def send(q, here, target, arrived):
            to_day, to_row = peer(q)
            pltpu.make_async_remote_copy(
                src_ref=send_b.at[k, to_day * rows + to_row, here, :],
                dst_ref=target,
                send_sem=b_send.at[k],
                recv_sem=arrived,
                device_id=(to_day, to_row),
                device_id_type=MESH,
            ).start()

        def send_part(n, first, count):
            tau, q = n // count, first + n % count
            here = block(tau, piece // SPLIT)
            send(q, here, recv_b.at[k, me, here, :], b_recv.at[k, tau // SPLIT])

        def send_last(n, first, count):
            i, q = n // count, first + n % count
            here = block((steps - 1) * parts + i, fine)
            send(q, here, recv_b.at[k, me, here, :], last_recv.at[i])

        def send_tail(q):
            send(q, block(steps * parts - 1, fine), tail.at[me], last_recv.at[parts - 1])

        @pl.when(k < chunks - 1)
        def _():
            each(steps * SPLIT * (peers - 1), lambda n: send_part(n, 0, peers - 1))

        @pl.when(k == chunks - 1)
        def _():
            far, near = peers // 2, peers - 1 - peers // 2
            each((steps - 1) * SPLIT * near, lambda n: send_part(n, far, near))
            each((parts - 1) * near, lambda n: send_last(n, far, near))
            each(near, lambda n: send_tail(far + n))
            each((steps - 1) * SPLIT * far, lambda n: send_part(n, 0, far))
            each((parts - 1) * far, lambda n: send_last(n, 0, far))
            each(far, lambda n: send_tail(far - 1 - n))

    each(chunks, middle)

    def clear(n):
        total[n // (height // TILE), block(n % (height // TILE), TILE), :] = jnp.zeros((TILE, order), jnp.float32)

    each(tiles * (height // TILE), clear)

    def along_b(k, tau, here, length, first, count, arrived):
        rest = recv_b.at[k, pl.ds(0, peers - 1), here, :]
        pltpu.make_async_copy(rest, rest, arrived).wait()
        load = pltpu.make_async_copy(recv_b.at[k, :, here, :], stage.at[:, pl.ds(0, length), :], local_sem)
        load.start()
        load.wait()

        def turn(i):
            high, low = split(stage[:, block(i, SUB), :].reshape(cols, own_rows).T)
            tall_high[block(i, own_rows), :] = high
            tall_low[block(i, own_rows), :] = low

        each(length // SUB, turn)

        def part(m):
            i, j = m // (order // TILE), m % (order // TILE)
            left = tall_high[block(i, TILE), :], tall_low[block(i, TILE), :]
            right = yt_high[k, :, block(j, TILE)], yt_low[k, :, block(j, TILE)]
            total[tau, block(first + i, TILE), block(j, TILE)] += dot3(left, right)

        each(count * (order // TILE), part)

    def backward(n):
        k, tau = n // steps, n % steps
        along_b(k, tau, block(tau, piece), piece, 0, parts, b_recv.at[k, tau])

    each(chunks * steps - 1, backward)

    def last(i):
        along_b(chunks - 1, steps - 1, block((steps - 1) * parts + i, fine), fine, i, 1, last_recv.at[i])

    each(parts - 1, last)
    rest = tail.at[pl.ds(0, peers - 1)]
    pltpu.make_async_copy(rest, rest, last_recv.at[parts - 1]).wait()

    def drain(k):
        sent = send_a.at[k, pl.ds(0, peers - 1)]
        pltpu.make_async_copy(sent, sent, a_send.at[k]).wait()
        sent = send_b.at[k, pl.ds(0, peers - 1)]
        pltpu.make_async_copy(sent, sent, b_send.at[k]).wait()

    each(chunks, drain)


def closing(total, tail, right_high, right_low, out, left_high, left_low, final, sems):
    steps, height, order = total.shape
    peers, fine, own_rows = tail.shape
    done = height - TILE
    copies = [
        pltpu.make_async_copy(total.at[tau], out.at[pl.ds(tau * height, height)], sems.at[tau])
        for tau in range(steps - 1)
    ]
    first = (steps - 1) * height
    copies.append(pltpu.make_async_copy(total.at[steps - 1, pl.ds(0, done)], out.at[pl.ds(first, done)], sems.at[steps - 1]))
    for copy in copies:
        copy.start()
    for i in range(fine // SUB):
        high, low = split(tail[:, i * SUB : (i + 1) * SUB, :].reshape(peers * SUB, own_rows).T)
        left_high[i * own_rows : (i + 1) * own_rows, :] = high
        left_low[i * own_rows : (i + 1) * own_rows, :] = low

    def part(j):
        here = block(j, TILE)
        value = dot3((left_high[...], left_low[...]), (right_high[:, here], right_low[:, here]))
        final[:, here] = total[steps - 1, pl.ds(done, TILE), here] + value

    each(order // TILE, part)
    copies.append(pltpu.make_async_copy(final, out.at[pl.ds(first + done, TILE)], sems.at[steps]))
    copies[-1].start()
    for copy in copies:
        copy.wait()


def fused(field, basis_day, basis_x, basis_y, eig_day, eig_x, eig_y, noise):
    own_days, own_rows, order = field.shape
    peers = lax.axis_size("day") * lax.axis_size("row")
    total_days = basis_day.shape[0]
    chunks = order // (peers * SUB)
    height = total_days * SUB
    span = height // own_rows
    steps = own_days // span
    depth = own_days * SUB
    f32, bf16 = jnp.float32, jnp.bfloat16
    wire = jax.ShapeDtypeStruct((chunks, peers, depth, own_rows), f32)
    anywhere = pl.BlockSpec(memory_space=pl.ANY)
    vmem = pl.BlockSpec(memory_space=pltpu.VMEM)
    cols = peers * SUB
    dma = pltpu.SemaphoreType.DMA
    square = pltpu.VMEM((order, order), bf16)
    small = pltpu.VMEM((total_days, total_days), bf16)
    result = pl.pallas_call(
        kernel,
        out_shape=(
            pltpu.VMEM((steps, height, order), f32),
            pltpu.VMEM((peers, TILE // own_rows * SUB, own_rows), f32),
            pltpu.VMEM((cols, order), bf16),
            pltpu.VMEM((cols, order), bf16),
            wire, wire, wire, wire,
        ),
        in_specs=[pl.BlockSpec(memory_space=pltpu.HBM)] * 8,
        out_specs=(vmem,) * 4 + (anywhere,) * 4,
        scratch_shapes=[
            pltpu.VMEM((chunks, order, cols), bf16),
            pltpu.VMEM((chunks, order, cols), bf16),
            pltpu.VMEM((chunks, cols, order), bf16),
            pltpu.VMEM((chunks, cols, order), bf16),
            square, square, square, square,
            small, small, small, small,
            pltpu.VMEM((total_days, total_days), f32),
            pltpu.VMEM((total_days, total_days), f32),
            pltpu.VMEM((1, total_days), f32),
            pltpu.VMEM((1, order), f32),
            pltpu.SMEM((order,), f32),
            pltpu.SMEM((1,), f32),
            pltpu.VMEM((order // LANES, height, LANES), f32),
            pltpu.VMEM((height, order), bf16),
            pltpu.VMEM((height, order), bf16),
            pltpu.VMEM((peers, span * SUB, own_rows), f32),
            pltpu.VMEM((height, cols), bf16),
            pltpu.VMEM((height, cols), bf16),
            dma((2, height // TILE)), dma((chunks,)), dma, dma((5,)), dma, dma, dma,
            dma((chunks,)), dma((chunks,)), dma((chunks,)), dma((chunks, steps)), dma((height // TILE,)),
        ],
        compiler_params=pltpu.CompilerParams(
            collective_id=0, has_side_effects=True, vmem_limit_bytes=44 * 1024 * 1024
        ),
    )(
        field.reshape(own_days * own_rows, order), basis_day, basis_x, basis_y,
        eig_day.reshape(1, -1), eig_x.reshape(1, -1), eig_y, noise,
    )
    return pl.pallas_call(
        closing,
        out_shape=jax.ShapeDtypeStruct((own_days * own_rows, order), f32),
        in_specs=[vmem] * 4,
        out_specs=anywhere,
        scratch_shapes=[
            pltpu.VMEM((TILE, cols), bf16),
            pltpu.VMEM((TILE, cols), bf16),
            pltpu.VMEM((TILE, order), f32),
            dma((steps + 1,)),
        ],
        compiler_params=pltpu.CompilerParams(vmem_limit_bytes=16 * 1024 * 1024),
    )(*result[:4]).reshape(field.shape)


def fits(field, basis_day, basis_x):
    own_days, own_rows, order = field.shape
    days, rows = lax.axis_size("day"), lax.axis_size("row")
    peers = days * rows
    height = basis_day.shape[0] * SUB
    return (
        days & (days - 1) == 0
        and rows & (rows - 1) == 0
        and own_rows == LANES
        and basis_day.shape[0] == LANES
        and order % (peers * SUB) == 0
        and peers * SUB == TILE
        and basis_x.shape[0] == order
        and height == order
        and own_days * own_rows == 4 * height
    )


def shift(block, axis, step):
    size = lax.axis_size(axis)
    if step % size == 0:
        return block
    return lax.ppermute(block, axis, [(i, (i + step) % size) for i in range(size)])


def rolled(array, dim, blocks, first, sign):
    width = array.shape[dim] // blocks
    starts = [((first + sign * j) % blocks) * width for j in range(blocks)]
    return jnp.concatenate([lax.dynamic_slice_in_dim(array, start, width, dim) for start in starts], axis=dim)


def exchanged(field, basis_day, basis_x, basis_y, eig_day, eig_x, eig_y, noise):
    precise = lax.Precision.HIGH
    days = lax.axis_size("day")
    rows = lax.axis_size("row")
    day = lax.axis_index("day")
    row = lax.axis_index("row")
    local_days, local_rows, grid_cols = field.shape
    grid_rows = basis_x.shape[0]
    own_cols = grid_cols // rows
    own_spec = grid_rows // days
    chunks = max(1, min(CHUNKS, own_cols // 32))
    width = own_cols // chunks

    def product(spec, left, right):
        return jnp.einsum(spec, left, right, precision=precise, preferred_element_type=jnp.float32)

    turn_x = rolled(rolled(basis_x, 0, rows, row, -1), 1, days, day, 1)
    turn_y = rolled(basis_y.T, 0, rows, row, 1).reshape(rows, chunks, width, grid_cols)
    turn_day = rolled(basis_day, 0, days, day, -1)
    part_x = lax.dynamic_slice_in_dim(eig_x, day * own_spec, own_spec)
    part_y = lax.dynamic_slice_in_dim(eig_y, row * own_cols, own_cols)
    parts = []
    for chunk in range(chunks):
        basis = turn_y[:, chunk].reshape(rows * width, grid_cols)
        along_y = product("by,txy->btx", basis, field)
        got = [shift(along_y[j * width : (j + 1) * width], "row", j) for j in range(rows)]
        along_x = product("btx,xa->bta", jnp.concatenate(got, axis=2), turn_x)
        got = [shift(along_x[:, :, j * own_spec : (j + 1) * own_spec], "day", j) for j in range(days)]
        spectral = product("ts,bta->bsa", turn_day, jnp.concatenate(got, axis=1))
        own_y = part_y[chunk * width : (chunk + 1) * width]
        spectrum = eig_day[None, :, None] * part_x[None, None, :] * own_y[:, None, None] + noise[0]
        back_day = product("ts,bsa->bta", turn_day, spectral / spectrum)
        got = [shift(back_day[:, j * local_days : (j + 1) * local_days], "day", -j) for j in range(days)]
        back_x = product("bta,xa->btx", jnp.concatenate(got, axis=2), turn_x)
        got = [shift(back_x[:, :, j * local_rows : (j + 1) * local_rows], "row", -j) for j in range(rows)]
        parts.append((basis, jnp.concatenate(got, axis=0)))
    weights = None
    for group in (parts[:-1], parts[-1:]):
        if group:
            basis = jnp.concatenate([g[0] for g in group], axis=0)
            value = product("btx,by->txy", jnp.concatenate([g[1] for g in group], axis=0), basis)
            weights = value if weights is None else weights + value
    return weights


def body(field, basis_day, basis_x, *rest):
    route = fused if fits(field, basis_day, basis_x) else exchanged
    return route(field, basis_day, basis_x, *rest)


def solution(mesh):
    in_specs = (P("day", "row", None), P(), P(), P(), P(), P(), P(), P())
    out_specs = P("day", "row", None)
    return jax.shard_map(body, mesh=mesh, in_specs=in_specs, out_specs=out_specs, check_vma=False)
```

```python
import functools
import jax
import jax.numpy as jnp
from jax import lax
from jax.experimental import pallas as pl
from jax.experimental.pallas import tpu as pltpu
from jax.sharding import PartitionSpec as P

CHUNKS = 4
SUB = 8
LANES = 128
TILE = 256
SPLIT = 2
MESH = pl.DeviceIdType.MESH


def split(value):
    high = value.astype(jnp.bfloat16)
    low = (value - high.astype(jnp.float32)).astype(jnp.bfloat16)
    return high, low


def dot3(left, right):
    def one(a, b):
        return jnp.dot(a, b, preferred_element_type=jnp.float32)

    return one(left[0], right[0]) + (one(left[0], right[1]) + one(left[1], right[0]))


def turns(index, size):
    return [bit * (1 - 2 * (index // bit % 2)) for bit in (1 << n for n in range(size.bit_length() - 1))]


def flipped(index, steps, mask):
    return index + sum((mask // (1 << n)) % 2 * step for n, step in enumerate(steps))


def block(start, size):
    return pl.ds(pl.multiple_of(start * size, size), size)


def each(count, fn):
    def step(i, carry):
        fn(i)
        return carry

    lax.fori_loop(0, count, step, 0)


def kernel(
    field, basis_day, basis_x, basis_y, day_values, x_values, y_values, noise_value,
    total, tail, last_high, last_low, send_a, recv_a, send_b, recv_b,
    y_high, y_low, yt_high, yt_low, x_high, x_low, xt_high, xt_low,
    day_high, day_low, dayt_high, dayt_low, day_col, day_full, eig_day, eig_x, eig_y, noise,
    sheets, left_high, left_low, stage, tall_high, tall_low,
    load_sem, y_sem, x_sem, small_sem, local_sem, own_sem, tail_sem,
    a_send, a_recv, b_send, b_recv, last_recv,
):
    days = lax.axis_size("day")
    rows = lax.axis_size("row")
    day = lax.axis_index("day")
    row = lax.axis_index("row")
    peers = days * rows
    me = day * rows + row
    chunks, _, depth, own_rows = recv_a.shape
    cols = peers * SUB
    tiles, height, order = total.shape[0], total.shape[1], total.shape[2]
    span = height // own_rows
    steps = depth // (span * SUB)
    piece = span * SUB
    total_days = basis_day.shape[0]

    day_turns, row_turns = turns(day, days), turns(row, rows)
    barrier = pltpu.get_barrier_semaphore()

    def peer(q):
        half = peers // 2
        near = q // half
        mask = (1 - near) * (half + q) + near * (peers - 1 - q)
        i, j = mask // days, mask % days
        return flipped(day, day_turns, j), flipped(row, row_turns, i)

    def greet():
        for mask in range(peers - 1, 0, -1):
            other = flipped(day, day_turns, mask % days), flipped(row, row_turns, mask // days)
            pl.semaphore_signal(barrier, inc=1, device_id=other, device_id_type=MESH)

    parts = height // TILE
    fine = piece // parts

    def load_part(n, i):
        source = field.at[block((n % steps) * parts + i, TILE)]
        return pltpu.make_async_copy(source, total.at[n % 2, block(i, TILE)], load_sem.at[n % 2, i])

    def load_field(n):
        each(parts, lambda i: load_part(n, i).start())

    def load_y(k):
        return pltpu.make_async_copy(basis_y.at[:, block(k, cols)], total.at[3, :, block(k, cols)], y_sem.at[k])

    load_y(0).start()
    load_part(0, 0).start()
    greet()
    load_x = pltpu.make_async_copy(basis_x, total.at[2], x_sem)
    loads = [
        pltpu.make_async_copy(source, target, small_sem.at[i])
        for i, (source, target) in enumerate(
            ((basis_day, day_full), (day_values, eig_day), (x_values, eig_x), (y_values, eig_y), (noise_value, noise))
        )
    ]

    def prepare_y(k):
        load_y(k).wait()

        def part(i):
            high, low = split(total[3, block(i, TILE), block(k, cols)])
            y_high[k, block(i, TILE), :] = high
            y_low[k, block(i, TILE), :] = low

        each(order // TILE, part)

    def split_rows(slot, first, count):
        def part(i):
            here = block(first * 4 + i, TILE // 4)
            high, low = split(total[slot, here, :])
            left_high[here, :] = high
            left_low[here, :] = low

        each(count * 4, part)

    def along_y(k, slot, first, count):
        split_rows(slot, first, count)

        def part(i):
            here = block(first + i, TILE)
            value = dot3((left_high[here, :], left_low[here, :]), (y_high[k], y_low[k])).T
            for j in range(TILE // own_rows):
                one = value[:, j * own_rows : (j + 1) * own_rows].reshape(peers, SUB, own_rows)
                stage[:, block(i * (TILE // own_rows) + j, SUB), :] = one

        each(count, part)

    def send_y(k, begin, length):
        here = block(begin, length)
        staged = stage.at[:, pl.ds(0, length), :]
        copy = pltpu.make_async_copy(staged, send_a.at[k, :, here, :], local_sem)
        own = pltpu.make_async_copy(stage.at[me, pl.ds(0, length), :], recv_a.at[k, me, here, :], own_sem)
        copy.start()
        own.start()
        copy.wait()
        count = SPLIT if length == piece else 1

        def send(m):
            q = m % (peers - 1)
            to_day, to_row = peer(q)
            where = pl.ds(pl.multiple_of(begin * length + m // (peers - 1) * (length // count), SUB), length // count)
            pltpu.make_async_remote_copy(
                src_ref=send_a.at[k, to_day * rows + to_row, where, :],
                dst_ref=recv_a.at[k, me, where, :],
                send_sem=a_send.at[k],
                recv_sem=a_recv.at[k],
                device_id=(to_day, to_row),
                device_id_type=MESH,
            ).start()

        each(count * (peers - 1), send)
        own.wait()

    prepare_y(0)
    load_part(0, 0).wait()
    each(parts - 1, lambda i: load_part(0, i + 1).start())
    along_y(0, 0, 0, 1)
    pl.semaphore_wait(barrier, peers - 1)
    send_y(0, 0, fine)
    load_field(1)
    each(chunks - 1, lambda k: load_y(k + 1).start())

    def first(i):
        load_part(0, i + 1).wait()
        along_y(0, 0, i + 1, 1)
        send_y(0, i + 1, fine)

    each(parts - 1, first)
    load_x.start()
    for load in loads:
        load.start()

    def forward(m):
        n = m + 1
        k = n // steps

        @pl.when(n % steps == 0)
        def _():
            prepare_y(k)

        each(parts, lambda i: load_part(n, i).wait())

        @pl.when(n + 1 < chunks * steps)
        def _():
            load_field(n + 1)

        along_y(k, n % 2, 0, parts)
        send_y(k, n % steps, piece)

    each(chunks * steps - 1, forward)

    for load in loads:
        load.wait()
    load_x.wait()

    def turn_y(k):
        def part(i):
            high, low = split(total[3, block(i, TILE), block(k, cols)].T)
            yt_high[k, :, block(i, TILE)] = high
            yt_low[k, :, block(i, TILE)] = low

        each(order // TILE, part)

    each(chunks, turn_y)

    def turn_x(i):
        def part(j):
            value = total[2, block(i, TILE), block(j, TILE)]
            high, low = split(value)
            x_high[block(i, TILE), block(j, TILE)] = high
            x_low[block(i, TILE), block(j, TILE)] = low
            high, low = split(value.T)
            xt_high[block(j, TILE), block(i, TILE)] = high
            xt_low[block(j, TILE), block(i, TILE)] = low

        each(order // TILE, part)

    each(order // TILE, turn_x)
    last_high[...] = yt_high[chunks - 1]
    last_low[...] = yt_low[chunks - 1]
    day_high[...], day_low[...] = split(day_full[...])
    dayt_high[...], dayt_low[...] = split(day_full[...].T)
    day_col[...] = jnp.broadcast_to(eig_day[...], (total_days, total_days)).T

    def spread(i, j, value):
        for part in range(TILE // LANES):
            sheets[j * (TILE // LANES) + part, block(i, TILE), :] = value[:, part * LANES : (part + 1) * LANES]

    def settle(i, j, value):
        total[2, block(i, TILE), block(j, TILE)] = value

    def product(put, high, low):
        def part(n):
            i, j = n // (order // TILE), n % (order // TILE)
            left = left_high[block(i, TILE), :], left_low[block(i, TILE), :]
            put(i, j, dot3(left, (high[:, block(j, TILE)], low[:, block(j, TILE)])))

        each((height // TILE) * (order // TILE), part)

    def middle(k):
        rest = recv_a.at[k, pl.ds(0, peers - 1)]
        pltpu.make_async_copy(rest, rest, a_recv.at[k]).wait()

        def gather(n):
            pltpu.make_async_copy(
                recv_a.at[k, n], total.at[0, block(n // rows, depth), block(n % rows, own_rows)], local_sem
            ).start()

        each(peers, gather)
        pltpu.make_async_copy(total.at[0], total.at[0], local_sem).wait()
        split_rows(0, 0, parts)
        product(spread, x_high, x_low)

        def solve(j):
            shape = eig_x[:, block(j, LANES)]
            for b in range(SUB):
                where = (j, pl.ds(b, total_days, stride=SUB), slice(None))
                spectral = dot3((dayt_high[...], dayt_low[...]), split(sheets[where]))
                level = eig_y[k * cols + me * SUB + b]
                scaled = spectral / (day_col[...] * shape * level + noise[0])
                sheets[where] = dot3((day_high[...], day_low[...]), split(scaled))

        each(order // LANES, solve)

        def rejoin(n):
            i, j = n // (order // LANES), n % (order // LANES)
            high, low = split(sheets[j, block(i, TILE), :])
            left_high[block(i, TILE), block(j, LANES)] = high
            left_low[block(i, TILE), block(j, LANES)] = low

        each((height // TILE) * (order // LANES), rejoin)
        product(settle, xt_high, xt_low)

        def scatter(n):
            pltpu.make_async_copy(
                total.at[2, block(n // rows, depth), block(n % rows, own_rows)], send_b.at[k, n], local_sem
            ).start()

        each(peers, scatter)
        own = pltpu.make_async_copy(total.at[2, block(day, depth), block(row, own_rows)], recv_b.at[k, me], own_sem)
        own.start()

        @pl.when(k == chunks - 1)
        def _():
            first = ((day + 1) * steps - 1) * parts
            copies = [
                pltpu.make_async_copy(
                    total.at[2, block(first + i, fine), block(row, own_rows)], tail.at[i, me], tail_sem.at[i]
                )
                for i in range(parts)
            ]
            for copy in copies:
                copy.start()
            for copy in copies:
                copy.wait()

        pltpu.make_async_copy(total.at[2], total.at[2], local_sem).wait()
        own.wait()

        def send(q, here, target, arrived):
            to_day, to_row = peer(q)
            pltpu.make_async_remote_copy(
                src_ref=send_b.at[k, to_day * rows + to_row, here, :],
                dst_ref=target,
                send_sem=b_send.at[k],
                recv_sem=arrived,
                device_id=(to_day, to_row),
                device_id_type=MESH,
            ).start()

        def send_part(n, first, count):
            tau, q = n // count, first + n % count
            here = block(tau, piece // SPLIT)
            send(q, here, recv_b.at[k, me, here, :], b_recv.at[k, tau // SPLIT])

        def send_last(n, first, count):
            i, q = n // count, first + n % count
            send(q, block((steps - 1) * parts + i, fine), tail.at[i, me], last_recv.at[i])

        def send_tail(q):
            send(q, block(steps * parts - 1, fine), tail.at[parts - 1, me], last_recv.at[parts - 1])

        @pl.when(k < chunks - 1)
        def _():
            each(steps * SPLIT * (peers - 1), lambda n: send_part(n, 0, peers - 1))

        @pl.when(k == chunks - 1)
        def _():
            far, near = peers // 2, peers - 1 - peers // 2
            each((steps - 1) * SPLIT * near, lambda n: send_part(n, far, near))
            each((parts - 1) * near, lambda n: send_last(n, far, near))
            each(near, lambda n: send_tail(far + n))
            each((steps - 1) * SPLIT * far, lambda n: send_part(n, 0, far))
            each((parts - 1) * far, lambda n: send_last(n, 0, far))
            each(far, lambda n: send_tail(far - 1 - n))

    each(chunks, middle)

    def clear(n):
        total[n // (height // TILE), block(n % (height // TILE), TILE), :] = jnp.zeros((TILE, order), jnp.float32)

    each(tiles * (height // TILE), clear)

    def along_b(k, tau, source, length, first, count):
        def turn(i):
            high, low = split(source[:, block(i, SUB), :].reshape(cols, own_rows).T)
            tall_high[block(i, own_rows), :] = high
            tall_low[block(i, own_rows), :] = low

        each(length // SUB, turn)

        def part(m):
            i, j = m // (order // TILE), m % (order // TILE)
            left = tall_high[block(i, TILE), :], tall_low[block(i, TILE), :]
            right = yt_high[k, :, block(j, TILE)], yt_low[k, :, block(j, TILE)]
            total[tau, block(first + i, TILE), block(j, TILE)] += dot3(left, right)

        each(count * (order // TILE), part)

    def backward(n):
        k, tau = n // steps, n % steps
        here = block(tau, piece)
        rest = recv_b.at[k, pl.ds(0, peers - 1), here, :]
        pltpu.make_async_copy(rest, rest, b_recv.at[k, tau]).wait()
        load = pltpu.make_async_copy(recv_b.at[k, :, here, :], stage, local_sem)
        load.start()
        load.wait()
        along_b(k, tau, stage, piece, 0, parts)

    each(chunks * steps - 1, backward)

    def arrive(i):
        rest = tail.at[i, pl.ds(0, peers - 1)]
        pltpu.make_async_copy(rest, rest, last_recv.at[i]).wait()

    def last(i):
        arrive(i)
        along_b(chunks - 1, steps - 1, tail.at[i], fine, i, 1)

    each(parts - 1, last)
    arrive(parts - 1)

    def drain(k):
        sent = send_a.at[k, pl.ds(0, peers - 1)]
        pltpu.make_async_copy(sent, sent, a_send.at[k]).wait()
        sent = send_b.at[k, pl.ds(0, peers - 1)]
        pltpu.make_async_copy(sent, sent, b_send.at[k]).wait()

    each(chunks, drain)


def closing(total, tail, right_high, right_low, out, left_high, left_low, final, sems):
    steps, height, order = total.shape
    parts, peers, fine, own_rows = tail.shape
    done = height - TILE
    copies = [
        pltpu.make_async_copy(total.at[tau], out.at[pl.ds(tau * height, height)], sems.at[tau])
        for tau in range(steps - 1)
    ]
    first = (steps - 1) * height
    copies.append(pltpu.make_async_copy(total.at[steps - 1, pl.ds(0, done)], out.at[pl.ds(first, done)], sems.at[steps - 1]))
    for copy in copies:
        copy.start()
    for i in range(fine // SUB):
        high, low = split(tail[parts - 1, :, i * SUB : (i + 1) * SUB, :].reshape(peers * SUB, own_rows).T)
        left_high[i * own_rows : (i + 1) * own_rows, :] = high
        left_low[i * own_rows : (i + 1) * own_rows, :] = low

    def part(j):
        here = block(j, TILE)
        value = dot3((left_high[...], left_low[...]), (right_high[:, here], right_low[:, here]))
        final[:, here] = total[steps - 1, pl.ds(done, TILE), here] + value

    each(order // TILE, part)
    copies.append(pltpu.make_async_copy(final, out.at[pl.ds(first + done, TILE)], sems.at[steps]))
    copies[-1].start()
    for copy in copies:
        copy.wait()


def fused(field, basis_day, basis_x, basis_y, eig_day, eig_x, eig_y, noise):
    own_days, own_rows, order = field.shape
    peers = lax.axis_size("day") * lax.axis_size("row")
    total_days = basis_day.shape[0]
    chunks = order // (peers * SUB)
    height = total_days * SUB
    span = height // own_rows
    steps = own_days // span
    depth = own_days * SUB
    f32, bf16 = jnp.float32, jnp.bfloat16
    wire = jax.ShapeDtypeStruct((chunks, peers, depth, own_rows), f32)
    anywhere = pl.BlockSpec(memory_space=pl.ANY)
    vmem = pl.BlockSpec(memory_space=pltpu.VMEM)
    cols = peers * SUB
    dma = pltpu.SemaphoreType.DMA
    square = pltpu.VMEM((order, order), bf16)
    small = pltpu.VMEM((total_days, total_days), bf16)
    result = pl.pallas_call(
        kernel,
        out_shape=(
            pltpu.VMEM((steps, height, order), f32),
            pltpu.VMEM((height // TILE, peers, TILE // own_rows * SUB, own_rows), f32),
            pltpu.VMEM((cols, order), bf16),
            pltpu.VMEM((cols, order), bf16),
            wire, wire, wire, wire,
        ),
        in_specs=[pl.BlockSpec(memory_space=pltpu.HBM)] * 8,
        out_specs=(vmem,) * 4 + (anywhere,) * 4,
        scratch_shapes=[
            pltpu.VMEM((chunks, order, cols), bf16),
            pltpu.VMEM((chunks, order, cols), bf16),
            pltpu.VMEM((chunks, cols, order), bf16),
            pltpu.VMEM((chunks, cols, order), bf16),
            square, square, square, square,
            small, small, small, small,
            pltpu.VMEM((total_days, total_days), f32),
            pltpu.VMEM((total_days, total_days), f32),
            pltpu.VMEM((1, total_days), f32),
            pltpu.VMEM((1, order), f32),
            pltpu.SMEM((order,), f32),
            pltpu.SMEM((1,), f32),
            pltpu.VMEM((order // LANES, height, LANES), f32),
            pltpu.VMEM((height, order), bf16),
            pltpu.VMEM((height, order), bf16),
            pltpu.VMEM((peers, span * SUB, own_rows), f32),
            pltpu.VMEM((height, cols), bf16),
            pltpu.VMEM((height, cols), bf16),
            dma((2, height // TILE)), dma((chunks,)), dma, dma((5,)), dma, dma, dma((height // TILE,)),
            dma((chunks,)), dma((chunks,)), dma((chunks,)), dma((chunks, steps)), dma((height // TILE,)),
        ],
        compiler_params=pltpu.CompilerParams(
            collective_id=0, has_side_effects=True, vmem_limit_bytes=44 * 1024 * 1024
        ),
    )(
        field.reshape(own_days * own_rows, order), basis_day, basis_x, basis_y,
        eig_day.reshape(1, -1), eig_x.reshape(1, -1), eig_y, noise,
    )
    return pl.pallas_call(
        closing,
        out_shape=jax.ShapeDtypeStruct((own_days * own_rows, order), f32),
        in_specs=[vmem] * 4,
        out_specs=anywhere,
        scratch_shapes=[
            pltpu.VMEM((TILE, cols), bf16),
            pltpu.VMEM((TILE, cols), bf16),
            pltpu.VMEM((TILE, order), f32),
            dma((steps + 1,)),
        ],
        compiler_params=pltpu.CompilerParams(vmem_limit_bytes=16 * 1024 * 1024),
    )(*result[:4]).reshape(field.shape)


def fits(field, basis_day, basis_x):
    own_days, own_rows, order = field.shape
    days, rows = lax.axis_size("day"), lax.axis_size("row")
    peers = days * rows
    height = basis_day.shape[0] * SUB
    return (
        days & (days - 1) == 0
        and rows & (rows - 1) == 0
        and own_rows == LANES
        and basis_day.shape[0] == LANES
        and order % (peers * SUB) == 0
        and peers * SUB == TILE
        and basis_x.shape[0] == order
        and height == order
        and own_days * own_rows == 4 * height
    )


def shift(block, axis, step):
    size = lax.axis_size(axis)
    if step % size == 0:
        return block
    return lax.ppermute(block, axis, [(i, (i + step) % size) for i in range(size)])


def rolled(array, dim, blocks, first, sign):
    width = array.shape[dim] // blocks
    starts = [((first + sign * j) % blocks) * width for j in range(blocks)]
    return jnp.concatenate([lax.dynamic_slice_in_dim(array, start, width, dim) for start in starts], axis=dim)


def exchanged(field, basis_day, basis_x, basis_y, eig_day, eig_x, eig_y, noise):
    precise = lax.Precision.HIGH
    days = lax.axis_size("day")
    rows = lax.axis_size("row")
    day = lax.axis_index("day")
    row = lax.axis_index("row")
    local_days, local_rows, grid_cols = field.shape
    grid_rows = basis_x.shape[0]
    own_cols = grid_cols // rows
    own_spec = grid_rows // days
    chunks = max(1, min(CHUNKS, own_cols // 32))
    width = own_cols // chunks

    def product(spec, left, right):
        return jnp.einsum(spec, left, right, precision=precise, preferred_element_type=jnp.float32)

    turn_x = rolled(rolled(basis_x, 0, rows, row, -1), 1, days, day, 1)
    turn_y = rolled(basis_y.T, 0, rows, row, 1).reshape(rows, chunks, width, grid_cols)
    turn_day = rolled(basis_day, 0, days, day, -1)
    part_x = lax.dynamic_slice_in_dim(eig_x, day * own_spec, own_spec)
    part_y = lax.dynamic_slice_in_dim(eig_y, row * own_cols, own_cols)
    parts = []
    for chunk in range(chunks):
        basis = turn_y[:, chunk].reshape(rows * width, grid_cols)
        along_y = product("by,txy->btx", basis, field)
        got = [shift(along_y[j * width : (j + 1) * width], "row", j) for j in range(rows)]
        along_x = product("btx,xa->bta", jnp.concatenate(got, axis=2), turn_x)
        got = [shift(along_x[:, :, j * own_spec : (j + 1) * own_spec], "day", j) for j in range(days)]
        spectral = product("ts,bta->bsa", turn_day, jnp.concatenate(got, axis=1))
        own_y = part_y[chunk * width : (chunk + 1) * width]
        spectrum = eig_day[None, :, None] * part_x[None, None, :] * own_y[:, None, None] + noise[0]
        back_day = product("ts,bsa->bta", turn_day, spectral / spectrum)
        got = [shift(back_day[:, j * local_days : (j + 1) * local_days], "day", -j) for j in range(days)]
        back_x = product("bta,xa->btx", jnp.concatenate(got, axis=2), turn_x)
        got = [shift(back_x[:, :, j * local_rows : (j + 1) * local_rows], "row", -j) for j in range(rows)]
        parts.append((basis, jnp.concatenate(got, axis=0)))
    weights = None
    for group in (parts[:-1], parts[-1:]):
        if group:
            basis = jnp.concatenate([g[0] for g in group], axis=0)
            value = product("btx,by->txy", jnp.concatenate([g[1] for g in group], axis=0), basis)
            weights = value if weights is None else weights + value
    return weights


def body(field, basis_day, basis_x, *rest):
    route = fused if fits(field, basis_day, basis_x) else exchanged
    return route(field, basis_day, basis_x, *rest)


def solution(mesh):
    in_specs = (P("day", "row", None), P(), P(), P(), P(), P(), P(), P())
    out_specs = P("day", "row", None)
    return jax.shard_map(body, mesh=mesh, in_specs=in_specs, out_specs=out_specs, check_vma=False)
```

```python
import functools
import jax
import jax.numpy as jnp
from jax import lax
from jax.experimental import pallas as pl
from jax.experimental.pallas import tpu as pltpu
from jax.sharding import PartitionSpec as P

CHUNKS = 4
SUB = 8
LANES = 128
TILE = 256
SPLIT = 2
MESH = pl.DeviceIdType.MESH


def split(value):
    high = value.astype(jnp.bfloat16)
    low = (value - high.astype(jnp.float32)).astype(jnp.bfloat16)
    return high, low


def dot3(left, right):
    def one(a, b):
        return jnp.dot(a, b, preferred_element_type=jnp.float32)

    return one(left[0], right[0]) + (one(left[0], right[1]) + one(left[1], right[0]))


def turns(index, size):
    return [bit * (1 - 2 * (index // bit % 2)) for bit in (1 << n for n in range(size.bit_length() - 1))]


def flipped(index, steps, mask):
    return index + sum((mask // (1 << n)) % 2 * step for n, step in enumerate(steps))


def block(start, size):
    return pl.ds(pl.multiple_of(start * size, size), size)


def each(count, fn):
    def step(i, carry):
        fn(i)
        return carry

    lax.fori_loop(0, count, step, 0)


def kernel(
    field, basis_day, basis_x, basis_y, day_values, x_values, y_values, noise_value,
    total, tail, last_high, last_low, send_a, recv_a, send_b, recv_b,
    y_high, y_low, yt_high, yt_low, x_high, x_low, xt_high, xt_low,
    day_high, day_low, dayt_high, dayt_low, day_col, day_full, eig_day, eig_x, eig_y, noise,
    sheets, left_high, left_low, stage, tall_high, tall_low,
    load_sem, y_sem, x_sem, small_sem, local_sem, own_sem, tail_sem,
    a_send, a_recv, b_send, b_recv, last_recv,
):
    days = lax.axis_size("day")
    rows = lax.axis_size("row")
    day = lax.axis_index("day")
    row = lax.axis_index("row")
    peers = days * rows
    me = day * rows + row
    chunks, _, depth, own_rows = recv_a.shape
    cols = peers * SUB
    tiles, height, order = total.shape[0], total.shape[1], total.shape[2]
    span = height // own_rows
    steps = depth // (span * SUB)
    piece = span * SUB
    total_days = basis_day.shape[0]

    day_turns, row_turns = turns(day, days), turns(row, rows)
    barrier = pltpu.get_barrier_semaphore()

    def peer(q):
        half = peers // 2
        near = q // half
        mask = (1 - near) * (half + q) + near * (peers - 1 - q)
        i, j = mask // days, mask % days
        return flipped(day, day_turns, j), flipped(row, row_turns, i)

    def greet():
        for mask in range(peers - 1, 0, -1):
            other = flipped(day, day_turns, mask % days), flipped(row, row_turns, mask // days)
            pl.semaphore_signal(barrier, inc=1, device_id=other, device_id_type=MESH)

    parts = height // TILE
    fine = piece // parts

    def load_part(n, i):
        source = field.at[block((n % steps) * parts + i, TILE)]
        return pltpu.make_async_copy(source, total.at[n % 2, block(i, TILE)], load_sem.at[n % 2, i])

    def load_field(n):
        each(parts, lambda i: load_part(n, i).start())

    def load_y(k):
        return pltpu.make_async_copy(basis_y.at[:, block(k, cols)], total.at[3, :, block(k, cols)], y_sem.at[k])

    load_y(0).start()
    load_part(0, 0).start()
    greet()
    load_x = pltpu.make_async_copy(basis_x, total.at[2], x_sem)
    loads = [
        pltpu.make_async_copy(source, target, small_sem.at[i])
        for i, (source, target) in enumerate(
            ((basis_day, day_full), (day_values, eig_day), (x_values, eig_x), (y_values, eig_y), (noise_value, noise))
        )
    ]

    def prepare_y(k):
        load_y(k).wait()

        def part(i):
            high, low = split(total[3, block(i, TILE), block(k, cols)])
            y_high[k, block(i, TILE), :] = high
            y_low[k, block(i, TILE), :] = low

        each(order // TILE, part)

    def split_rows(slot, first, count):
        def part(i):
            here = block(first * 4 + i, TILE // 4)
            high, low = split(total[slot, here, :])
            left_high[here, :] = high
            left_low[here, :] = low

        each(count * 4, part)

    def along_y(k, slot, first, count):
        split_rows(slot, first, count)

        def part(i):
            here = block(first + i, TILE)
            value = dot3((left_high[here, :], left_low[here, :]), (y_high[k], y_low[k])).T
            for j in range(TILE // own_rows):
                one = value[:, j * own_rows : (j + 1) * own_rows].reshape(peers, SUB, own_rows)
                stage[:, block(i * (TILE // own_rows) + j, SUB), :] = one

        each(count, part)

    def send_y(k, begin, length, entry=False):
        here = block(begin, length)
        staged = stage.at[:, pl.ds(0, length), :]
        copy = pltpu.make_async_copy(staged, send_a.at[k, :, here, :], local_sem)
        own = pltpu.make_async_copy(stage.at[me, pl.ds(0, length), :], recv_a.at[k, me, here, :], own_sem)
        copy.start()
        own.start()
        copy.wait()
        if entry:
            pl.semaphore_wait(barrier, peers - 1)
        count = SPLIT if length == piece else 1

        def send(m):
            q = m % (peers - 1)
            to_day, to_row = peer(q)
            where = pl.ds(pl.multiple_of(begin * length + m // (peers - 1) * (length // count), SUB), length // count)
            pltpu.make_async_remote_copy(
                src_ref=send_a.at[k, to_day * rows + to_row, where, :],
                dst_ref=recv_a.at[k, me, where, :],
                send_sem=a_send.at[k],
                recv_sem=a_recv.at[k],
                device_id=(to_day, to_row),
                device_id_type=MESH,
            ).start()

        each(count * (peers - 1), send)
        own.wait()

    prepare_y(0)
    load_part(0, 0).wait()
    each(parts - 1, lambda i: load_part(0, i + 1).start())
    along_y(0, 0, 0, 1)
    send_y(0, 0, fine, True)
    load_field(1)
    each(chunks - 1, lambda k: load_y(k + 1).start())

    def first(i):
        load_part(0, i + 1).wait()
        along_y(0, 0, i + 1, 1)
        send_y(0, i + 1, fine)

    each(parts - 1, first)
    load_x.start()
    for load in loads:
        load.start()

    def forward(m):
        n = m + 1
        k = n // steps

        @pl.when(n % steps == 0)
        def _():
            prepare_y(k)

        each(parts, lambda i: load_part(n, i).wait())

        @pl.when(n + 1 < chunks * steps)
        def _():
            load_field(n + 1)

        along_y(k, n % 2, 0, parts)
        send_y(k, n % steps, piece)

    each(chunks * steps - 1, forward)

    for load in loads:
        load.wait()
    load_x.wait()

    def turn_y(k):
        def part(i):
            high, low = split(total[3, block(i, TILE), block(k, cols)].T)
            yt_high[k, :, block(i, TILE)] = high
            yt_low[k, :, block(i, TILE)] = low

        each(order // TILE, part)

    each(chunks, turn_y)

    def turn_x(i):
        def part(j):
            value = total[2, block(i, TILE), block(j, TILE)]
            high, low = split(value)
            x_high[block(i, TILE), block(j, TILE)] = high
            x_low[block(i, TILE), block(j, TILE)] = low
            high, low = split(value.T)
            xt_high[block(j, TILE), block(i, TILE)] = high
            xt_low[block(j, TILE), block(i, TILE)] = low

        each(order // TILE, part)

    each(order // TILE, turn_x)
    last_high[...] = yt_high[chunks - 1]
    last_low[...] = yt_low[chunks - 1]
    day_high[...], day_low[...] = split(day_full[...])
    dayt_high[...], dayt_low[...] = split(day_full[...].T)
    day_col[...] = jnp.broadcast_to(eig_day[...], (total_days, total_days)).T

    def spread(i, j, value):
        for part in range(TILE // LANES):
            sheets[j * (TILE // LANES) + part, block(i, TILE), :] = value[:, part * LANES : (part + 1) * LANES]

    def settle(i, j, value):
        total[2, block(i, TILE), block(j, TILE)] = value

    def product(put, high, low):
        def part(n):
            i, j = n // (order // TILE), n % (order // TILE)
            left = left_high[block(i, TILE), :], left_low[block(i, TILE), :]
            put(i, j, dot3(left, (high[:, block(j, TILE)], low[:, block(j, TILE)])))

        each((height // TILE) * (order // TILE), part)

    def middle(k):
        rest = recv_a.at[k, pl.ds(0, peers - 1)]
        pltpu.make_async_copy(rest, rest, a_recv.at[k]).wait()

        def gather(n):
            pltpu.make_async_copy(
                recv_a.at[k, n], total.at[0, block(n // rows, depth), block(n % rows, own_rows)], local_sem
            ).start()

        each(peers, gather)
        pltpu.make_async_copy(total.at[0], total.at[0], local_sem).wait()
        split_rows(0, 0, parts)
        product(spread, x_high, x_low)

        def solve(j):
            shape = eig_x[:, block(j, LANES)]
            for b in range(SUB):
                where = (j, pl.ds(b, total_days, stride=SUB), slice(None))
                spectral = dot3((dayt_high[...], dayt_low[...]), split(sheets[where]))
                level = eig_y[k * cols + me * SUB + b]
                scaled = spectral / (day_col[...] * shape * level + noise[0])
                sheets[where] = dot3((day_high[...], day_low[...]), split(scaled))

        each(order // LANES, solve)

        def rejoin(n):
            i, j = n // (order // LANES), n % (order // LANES)
            high, low = split(sheets[j, block(i, TILE), :])
            left_high[block(i, TILE), block(j, LANES)] = high
            left_low[block(i, TILE), block(j, LANES)] = low

        each((height // TILE) * (order // LANES), rejoin)
        product(settle, xt_high, xt_low)

        def scatter(n):
            pltpu.make_async_copy(
                total.at[2, block(n // rows, depth), block(n % rows, own_rows)], send_b.at[k, n], local_sem
            ).start()

        each(peers, scatter)
        own = pltpu.make_async_copy(total.at[2, block(day, depth), block(row, own_rows)], recv_b.at[k, me], own_sem)
        own.start()

        @pl.when(k == chunks - 1)
        def _():
            first = ((day + 1) * steps - 1) * parts
            copies = [
                pltpu.make_async_copy(
                    total.at[2, block(first + i, fine), block(row, own_rows)], tail.at[i, me], tail_sem.at[i]
                )
                for i in range(parts)
            ]
            for copy in copies:
                copy.start()
            for copy in copies:
                copy.wait()

        pltpu.make_async_copy(total.at[2], total.at[2], local_sem).wait()
        own.wait()

        def send(q, here, target, arrived):
            to_day, to_row = peer(q)
            pltpu.make_async_remote_copy(
                src_ref=send_b.at[k, to_day * rows + to_row, here, :],
                dst_ref=target,
                send_sem=b_send.at[k],
                recv_sem=arrived,
                device_id=(to_day, to_row),
                device_id_type=MESH,
            ).start()

        def send_part(n, first, count):
            tau, q = n // count, first + n % count
            here = block(tau, piece // SPLIT)
            send(q, here, recv_b.at[k, me, here, :], b_recv.at[k, tau // SPLIT])

        def send_last(n, first, count):
            i, q = n // count, first + n % count
            send(q, block((steps - 1) * parts + i, fine), tail.at[i, me], last_recv.at[i])

        def send_tail(q):
            send(q, block(steps * parts - 1, fine), tail.at[parts - 1, me], last_recv.at[parts - 1])

        @pl.when(k < chunks - 1)
        def _():
            each(steps * SPLIT * (peers - 1), lambda n: send_part(n, 0, peers - 1))

        @pl.when(k == chunks - 1)
        def _():
            far, near = peers // 2, peers - 1 - peers // 2
            each((steps - 1) * SPLIT * near, lambda n: send_part(n, far, near))
            each((parts - 1) * near, lambda n: send_last(n, far, near))
            each(near, lambda n: send_tail(far + n))
            each((steps - 1) * SPLIT * far, lambda n: send_part(n, 0, far))
            each((parts - 1) * far, lambda n: send_last(n, 0, far))
            each(far, lambda n: send_tail(far - 1 - n))

    each(chunks, middle)

    def clear(n):
        total[n // (height // TILE), block(n % (height // TILE), TILE), :] = jnp.zeros((TILE, order), jnp.float32)

    each(tiles * (height // TILE), clear)

    def along_b(k, tau, source, length, first, count):
        def turn(i):
            high, low = split(source[:, block(i, SUB), :].reshape(cols, own_rows).T)
            tall_high[block(i, own_rows), :] = high
            tall_low[block(i, own_rows), :] = low

        each(length // SUB, turn)

        def part(m):
            i, j = m // (order // TILE), m % (order // TILE)
            left = tall_high[block(i, TILE), :], tall_low[block(i, TILE), :]
            right = yt_high[k, :, block(j, TILE)], yt_low[k, :, block(j, TILE)]
            total[tau, block(first + i, TILE), block(j, TILE)] += dot3(left, right)

        each(count * (order // TILE), part)

    def backward(n):
        k, tau = n // steps, n % steps
        here = block(tau, piece)
        rest = recv_b.at[k, pl.ds(0, peers - 1), here, :]
        pltpu.make_async_copy(rest, rest, b_recv.at[k, tau]).wait()
        load = pltpu.make_async_copy(recv_b.at[k, :, here, :], stage, local_sem)
        load.start()
        load.wait()
        along_b(k, tau, stage, piece, 0, parts)

    each(chunks * steps - 1, backward)

    def arrive(i):
        rest = tail.at[i, pl.ds(0, peers - 1)]
        pltpu.make_async_copy(rest, rest, last_recv.at[i]).wait()

    def last(i):
        arrive(i)
        along_b(chunks - 1, steps - 1, tail.at[i], fine, i, 1)

    each(parts - 1, last)
    arrive(parts - 1)

    def drain(k):
        sent = send_a.at[k, pl.ds(0, peers - 1)]
        pltpu.make_async_copy(sent, sent, a_send.at[k]).wait()
        sent = send_b.at[k, pl.ds(0, peers - 1)]
        pltpu.make_async_copy(sent, sent, b_send.at[k]).wait()

    each(chunks, drain)


def closing(total, tail, right_high, right_low, out, left_high, left_low, final, sems):
    steps, height, order = total.shape
    parts, peers, fine, own_rows = tail.shape
    done = height - TILE
    copies = [
        pltpu.make_async_copy(total.at[tau], out.at[pl.ds(tau * height, height)], sems.at[tau])
        for tau in range(steps - 1)
    ]
    first = (steps - 1) * height
    copies.append(pltpu.make_async_copy(total.at[steps - 1, pl.ds(0, done)], out.at[pl.ds(first, done)], sems.at[steps - 1]))
    for copy in copies:
        copy.start()
    for i in range(fine // SUB):
        high, low = split(tail[parts - 1, :, i * SUB : (i + 1) * SUB, :].reshape(peers * SUB, own_rows).T)
        left_high[i * own_rows : (i + 1) * own_rows, :] = high
        left_low[i * own_rows : (i + 1) * own_rows, :] = low

    def part(j):
        here = block(j, TILE)
        value = dot3((left_high[...], left_low[...]), (right_high[:, here], right_low[:, here]))
        final[:, here] = total[steps - 1, pl.ds(done, TILE), here] + value

    each(order // TILE, part)
    copies.append(pltpu.make_async_copy(final, out.at[pl.ds(first + done, TILE)], sems.at[steps]))
    copies[-1].start()
    for copy in copies:
        copy.wait()


def fused(field, basis_day, basis_x, basis_y, eig_day, eig_x, eig_y, noise):
    own_days, own_rows, order = field.shape
    peers = lax.axis_size("day") * lax.axis_size("row")
    total_days = basis_day.shape[0]
    chunks = order // (peers * SUB)
    height = total_days * SUB
    span = height // own_rows
    steps = own_days // span
    depth = own_days * SUB
    f32, bf16 = jnp.float32, jnp.bfloat16
    wire = jax.ShapeDtypeStruct((chunks, peers, depth, own_rows), f32)
    anywhere = pl.BlockSpec(memory_space=pl.ANY)
    vmem = pl.BlockSpec(memory_space=pltpu.VMEM)
    cols = peers * SUB
    dma = pltpu.SemaphoreType.DMA
    square = pltpu.VMEM((order, order), bf16)
    small = pltpu.VMEM((total_days, total_days), bf16)
    result = pl.pallas_call(
        kernel,
        out_shape=(
            pltpu.VMEM((steps, height, order), f32),
            pltpu.VMEM((height // TILE, peers, TILE // own_rows * SUB, own_rows), f32),
            pltpu.VMEM((cols, order), bf16),
            pltpu.VMEM((cols, order), bf16),
            wire, wire, wire, wire,
        ),
        in_specs=[pl.BlockSpec(memory_space=pltpu.HBM)] * 8,
        out_specs=(vmem,) * 4 + (anywhere,) * 4,
        scratch_shapes=[
            pltpu.VMEM((chunks, order, cols), bf16),
            pltpu.VMEM((chunks, order, cols), bf16),
            pltpu.VMEM((chunks, cols, order), bf16),
            pltpu.VMEM((chunks, cols, order), bf16),
            square, square, square, square,
            small, small, small, small,
            pltpu.VMEM((total_days, total_days), f32),
            pltpu.VMEM((total_days, total_days), f32),
            pltpu.VMEM((1, total_days), f32),
            pltpu.VMEM((1, order), f32),
            pltpu.SMEM((order,), f32),
            pltpu.SMEM((1,), f32),
            pltpu.VMEM((order // LANES, height, LANES), f32),
            pltpu.VMEM((height, order), bf16),
            pltpu.VMEM((height, order), bf16),
            pltpu.VMEM((peers, span * SUB, own_rows), f32),
            pltpu.VMEM((height, cols), bf16),
            pltpu.VMEM((height, cols), bf16),
            dma((2, height // TILE)), dma((chunks,)), dma, dma((5,)), dma, dma, dma((height // TILE,)),
            dma((chunks,)), dma((chunks,)), dma((chunks,)), dma((chunks, steps)), dma((height // TILE,)),
        ],
        compiler_params=pltpu.CompilerParams(
            collective_id=0, has_side_effects=True, vmem_limit_bytes=44 * 1024 * 1024
        ),
    )(
        field.reshape(own_days * own_rows, order), basis_day, basis_x, basis_y,
        eig_day.reshape(1, -1), eig_x.reshape(1, -1), eig_y, noise,
    )
    return pl.pallas_call(
        closing,
        out_shape=jax.ShapeDtypeStruct((own_days * own_rows, order), f32),
        in_specs=[vmem] * 4,
        out_specs=anywhere,
        scratch_shapes=[
            pltpu.VMEM((TILE, cols), bf16),
            pltpu.VMEM((TILE, cols), bf16),
            pltpu.VMEM((TILE, order), f32),
            dma((steps + 1,)),
        ],
        compiler_params=pltpu.CompilerParams(vmem_limit_bytes=16 * 1024 * 1024),
    )(*result[:4]).reshape(field.shape)


def fits(field, basis_day, basis_x):
    own_days, own_rows, order = field.shape
    days, rows = lax.axis_size("day"), lax.axis_size("row")
    peers = days * rows
    height = basis_day.shape[0] * SUB
    return (
        days & (days - 1) == 0
        and rows & (rows - 1) == 0
        and own_rows == LANES
        and basis_day.shape[0] == LANES
        and order % (peers * SUB) == 0
        and peers * SUB == TILE
        and basis_x.shape[0] == order
        and height == order
        and own_days * own_rows == 4 * height
    )


def shift(block, axis, step):
    size = lax.axis_size(axis)
    if step % size == 0:
        return block
    return lax.ppermute(block, axis, [(i, (i + step) % size) for i in range(size)])


def rolled(array, dim, blocks, first, sign):
    width = array.shape[dim] // blocks
    starts = [((first + sign * j) % blocks) * width for j in range(blocks)]
    return jnp.concatenate([lax.dynamic_slice_in_dim(array, start, width, dim) for start in starts], axis=dim)


def exchanged(field, basis_day, basis_x, basis_y, eig_day, eig_x, eig_y, noise):
    precise = lax.Precision.HIGH
    days = lax.axis_size("day")
    rows = lax.axis_size("row")
    day = lax.axis_index("day")
    row = lax.axis_index("row")
    local_days, local_rows, grid_cols = field.shape
    grid_rows = basis_x.shape[0]
    own_cols = grid_cols // rows
    own_spec = grid_rows // days
    chunks = max(1, min(CHUNKS, own_cols // 32))
    width = own_cols // chunks

    def product(spec, left, right):
        return jnp.einsum(spec, left, right, precision=precise, preferred_element_type=jnp.float32)

    turn_x = rolled(rolled(basis_x, 0, rows, row, -1), 1, days, day, 1)
    turn_y = rolled(basis_y.T, 0, rows, row, 1).reshape(rows, chunks, width, grid_cols)
    turn_day = rolled(basis_day, 0, days, day, -1)
    part_x = lax.dynamic_slice_in_dim(eig_x, day * own_spec, own_spec)
    part_y = lax.dynamic_slice_in_dim(eig_y, row * own_cols, own_cols)
    parts = []
    for chunk in range(chunks):
        basis = turn_y[:, chunk].reshape(rows * width, grid_cols)
        along_y = product("by,txy->btx", basis, field)
        got = [shift(along_y[j * width : (j + 1) * width], "row", j) for j in range(rows)]
        along_x = product("btx,xa->bta", jnp.concatenate(got, axis=2), turn_x)
        got = [shift(along_x[:, :, j * own_spec : (j + 1) * own_spec], "day", j) for j in range(days)]
        spectral = product("ts,bta->bsa", turn_day, jnp.concatenate(got, axis=1))
        own_y = part_y[chunk * width : (chunk + 1) * width]
        spectrum = eig_day[None, :, None] * part_x[None, None, :] * own_y[:, None, None] + noise[0]
        back_day = product("ts,bsa->bta", turn_day, spectral / spectrum)
        got = [shift(back_day[:, j * local_days : (j + 1) * local_days], "day", -j) for j in range(days)]
        back_x = product("bta,xa->btx", jnp.concatenate(got, axis=2), turn_x)
        got = [shift(back_x[:, :, j * local_rows : (j + 1) * local_rows], "row", -j) for j in range(rows)]
        parts.append((basis, jnp.concatenate(got, axis=0)))
    weights = None
    for group in (parts[:-1], parts[-1:]):
        if group:
            basis = jnp.concatenate([g[0] for g in group], axis=0)
            value = product("btx,by->txy", jnp.concatenate([g[1] for g in group], axis=0), basis)
            weights = value if weights is None else weights + value
    return weights


def body(field, basis_day, basis_x, *rest):
    route = fused if fits(field, basis_day, basis_x) else exchanged
    return route(field, basis_day, basis_x, *rest)


def solution(mesh):
    in_specs = (P("day", "row", None), P(), P(), P(), P(), P(), P(), P())
    out_specs = P("day", "row", None)
    return jax.shard_map(body, mesh=mesh, in_specs=in_specs, out_specs=out_specs, check_vma=False)
```
